32 devices in a mesh: orient: 4 (over z), dom: 2 (over core), shell: 4 (over y, x).
Axes of the slice: x: 2, y: 2, z: 4, core: 2. Of those that a mesh axis runs over, the one named last changes fastest.
Arguments:
- references: bfloat16 [2048, 2, 4096], P('orient', None, 'shell'), may hold values from -6 to 6
- images: bfloat16 [512, 2, 4096], P(('orient', 'dom'), None, 'shell'), may hold values from -20 to 20
- noise_var: float32 [64], replicated, may hold values from 32 to 128
- shell_of: int32 [4096], P('shell'), may hold values from 0 to 63, never falling along the last dimension, each value on 1 to 128 neighbouring positions
- kept_blocks: int32 [4, 2, 3], P('orient', 'dom'), may hold values from -1 to 3, as said below
Outputs:
- weighted: float32 [2048, 2, 4096], P(('orient', 'dom'), None, 'shell')
- log_norm: float32 [512], P(('orient', 'dom'))
The draws below stay inside these ranges and needn't reach their ends.
Inputs may be any that keep to these rules, and one draw needn't show every extreme that they name: `kept_blocks`: each list holds distinct block numbers first, then -1 entries; the list of orientation block o and group d always starts with o; some list holds 3 blocks.
All inputs are finite; a program needn't handle non-finite values.
Results may differ from the reference program's by a relative error of at most 0.0051.
Values may be sent and summed in bfloat16 or wider, within the bound.
A program may use at most 64 MiB of HBM per device.

```python
import math
import jax
import jax.numpy as jnp
import numpy as np
from jax import lax

K = 4096
SHELLS = 64
OR_DEV = 512
IMG_DEV = 64
SHELL_MOST = 128
OBLK = 4
GROUPS = 2
MOST = 3
ORIENT = 2048
IMAGES = 512


def reference_values(key):
    base_key = jax.random.fold_in(key, 101)
    second = jax.random.fold_in(base_key, 1)
    values = jax.random.normal(second, (ORIENT, 2, K))
    return jnp.clip(values, -6.0, 6.0)


def draw_references(key, part):
    return reference_values(key).astype(jnp.bfloat16)


def draw_images(key, part):
    image_key = jax.random.fold_in(key, 202)
    second = jax.random.fold_in(image_key, 1)
    values = jax.random.normal(second, (IMAGES, 2, K))
    return jnp.clip(values, -20.0, 20.0).astype(jnp.bfloat16)


def draw_kept_blocks(key, part):
    list_key = jax.random.fold_in(key, 303)
    first, second, third = jax.random.split(list_key, 3)
    ranks = jax.random.randint(first, (OBLK, GROUPS, OBLK), 0, 1 << 20) * OBLK + jnp.arange(OBLK, dtype=jnp.int32)[None, None, :]
    itself = jnp.arange(OBLK, dtype=jnp.int32)[:, None, None] == jnp.arange(OBLK, dtype=jnp.int32)[None, None, :]
    ranks = jnp.where(itself, -1, ranks)
    order = jnp.argsort(ranks, axis=-1, stable=True)[:, :, :MOST].astype(jnp.int32)
    counts = jax.random.randint(second, (OBLK, GROUPS), 1, MOST + 1)
    chosen_row = jax.random.randint(third, (), 0, OBLK * GROUPS)
    counts = jnp.where(jnp.arange(OBLK * GROUPS, dtype=jnp.int32).reshape(OBLK, GROUPS) == chosen_row, MOST, counts)
    places = jnp.arange(MOST, dtype=jnp.int32)
    return jnp.where(places[None, None, :] < counts[:, :, None], order, -1).astype(jnp.int32)


def split_up(number_of, total, limit, lean):
    weights = [(1 << 20) // math.isqrt(rank ** lean) + 1 for rank in range(2, number_of + 1)]
    rest, given = total - limit - (number_of - 1), [1] * (number_of - 1)
    while rest > 0:
        free = [i for i in range(number_of - 1) if given[i] < limit]
        whole, budget = sum([weights[i] for i in free]), rest
        for i in free:
            more = min(limit - given[i], max(1, budget * weights[i] // whole), rest)
            given[i] = given[i] + more
            rest = rest - more
    return np.array([limit] + given)


def uneven_parts(key, amount, total, limit, skew):
    if amount == 2:
        one = jax.random.randint(key, (), max(1, total - limit), min(limit, total - 1) + 1)
        return jnp.stack([one, total - one])
    sizes = jnp.asarray(split_up(amount, total, limit, skew), jnp.int32)
    pairs = (amount - 1) // 2
    donor, taker = sizes[1:1 + 2 * pairs:2], sizes[2:2 + 2 * pairs:2]
    slack = jnp.minimum(donor - 1, limit - taker)
    passed = jax.random.randint(jax.random.fold_in(key, 1), (pairs,), 0, 1 << 20) % (slack + 1)
    sizes = sizes.at[1:1 + 2 * pairs:2].set(donor - passed).at[2:2 + 2 * pairs:2].set(taker + passed)
    return sizes[jax.random.permutation(jax.random.fold_in(key, 2), amount)]


def setup_inputs(seed: int = 0) -> dict:
    keys = jax.random.split(jax.random.key(seed), 6)
    return {
        "references": draw_references(jax.random.fold_in(keys[5], 71), 0),
        "images": draw_images(jax.random.fold_in(keys[5], 71), 0),
        "noise_var": jnp.clip(jnp.exp(jax.random.uniform(keys[2], (SHELLS,), jnp.float32, math.log(32.0), math.log(128.0))), 32.0, 128.0),
        "shell_of": jnp.searchsorted(jnp.cumsum(uneven_parts(keys[3], SHELLS, K, SHELL_MOST, 1)), jnp.arange(K), side="right").astype(jnp.int32),
        "kept_blocks": draw_kept_blocks(jax.random.fold_in(keys[5], 71), 0),
    }


floor_value = -1e30


def reference(references, images, noise_var, shell_of, kept_blocks):
    blocks = kept_blocks.shape[0]
    groups = kept_blocks.shape[1]
    coef_weight = 1.0 / noise_var[shell_of]
    scaled = (images.astype(jnp.float32) * coef_weight).astype(jnp.bfloat16)
    scaled_flat = scaled.reshape(IMAGES, 2 * K)
    both_weight = jnp.concatenate([coef_weight, coef_weight])
    found = jnp.any(kept_blocks[:, :, :, None] == jnp.arange(blocks, dtype=jnp.int32)[None, None, None, :], axis=2)
    keep_image = jnp.repeat(jnp.transpose(found, (0, 2, 1)).reshape(blocks, blocks * groups), IMG_DEV, axis=1)
    ref_blocks = references.reshape(blocks, OR_DEV, 2 * K)

    def block_scores(inputs):
        ref_rows, keep_row = inputs
        cross = lax.dot_general(ref_rows, scaled_flat, (((1,), (1,)), ((), ())), preferred_element_type=jnp.float32)
        ref_norm = jnp.sum(both_weight[None, :] * jnp.square(ref_rows.astype(jnp.float32)), axis=1)
        value = cross - 0.5 * ref_norm[:, None]
        return jnp.where(keep_row[None, :], value, floor_value)

    scores = lax.map(block_scores, (ref_blocks, keep_image))
    keep_full = keep_image[:, None, :]
    highest = jnp.max(scores, axis=(0, 1))
    total_mass = jnp.sum(jnp.where(keep_full, jnp.exp(scores - highest[None, None, :]), 0.0), axis=(0, 1))
    log_norm = highest + jnp.log(total_mass)
    posterior = jnp.where(keep_full, jnp.exp(scores - log_norm[None, None, :]), 0.0).astype(jnp.bfloat16)
    images_flat = images.reshape(IMAGES, 2 * K)

    def block_sums(post_rows):
        return jnp.dot(post_rows, images_flat, preferred_element_type=jnp.float32)

    weighted = lax.map(block_sums, posterior).reshape(ORIENT, 2, K)
    return weighted, log_norm
```

```python
import functools

import jax
import jax.numpy as jnp
from jax import lax
from jax.experimental import pallas as pl
from jax.experimental.pallas import tpu as pltpu
from jax.sharding import PartitionSpec as P

floor_value = -1e30
MESH = pl.DeviceIdType.MESH


def kernel(
    sizes, kept_ref, noise_ref, shell_ref, refs_ref, img_ref, out_ref, logn_ref,
    images, part, recvp, ebuf, abuf, erecv, lstat, zstat, w_s, rn_s,
    up_sem, dn_sem, img_sem, dom_send, dom_recv, rs_send, rs_recv,
    st_send, st_recv, e_send, e_recv, z_send, z_recv,
):
    O, D, S = sizes
    z, d, s = lax.axis_index("orient"), lax.axis_index("dom"), lax.axis_index("shell")
    rows = refs_ref.shape[0]
    img_rows = img_ref.shape[0]
    lanes = rows // S
    per = S // D
    most = kept_ref.shape[0]
    owner = s // per
    slot = s % per

    def dev(a, b, c):
        return {"orient": a, "dom": b, "shell": c}

    barrier = pltpu.get_barrier_semaphore()
    for o in range(1, O):
        pl.semaphore_signal(barrier, inc=1, device_id=dev(lax.rem(z + o, O), d, s), device_id_type=MESH)
    for od in range(D):
        for os in range(S):
            if od or os:
                pl.semaphore_signal(
                    barrier, inc=1,
                    device_id=dev(z, lax.rem(d + od, D), lax.rem(s + os, S)),
                    device_id_type=MESH,
                )
    pl.semaphore_wait(barrier, O - 1 + D * S - 1)

    def up(src, j):
        return pltpu.make_async_remote_copy(
            src_ref=src, dst_ref=images.at[d, j], send_sem=up_sem.at[j], recv_sem=img_sem.at[j],
            device_id=dev(lax.rem(z + 1, O), d, s), device_id_type=MESH)

    def down(src, j):
        return pltpu.make_async_remote_copy(
            src_ref=src, dst_ref=images.at[d, j], send_sem=dn_sem.at[j], recv_sem=img_sem.at[j],
            device_id=dev(lax.rem(z + O - 1, O), d, s), device_id_type=MESH)

    def across(src, od, j):
        return pltpu.make_async_remote_copy(
            src_ref=src, dst_ref=images.at[d, j], send_sem=dom_send.at[od, j],
            recv_sem=dom_recv.at[od, j],
            device_id=dev(z, lax.rem(d + od, D), s), device_id_type=MESH)

    def scatter(j, o):
        to = lax.rem(s + o, S)
        return pltpu.make_async_remote_copy(
            src_ref=part.at[j, to], dst_ref=recvp.at[j, o], send_sem=rs_send.at[j, o],
            recv_sem=rs_recv.at[j, o], device_id=dev(z, d, to), device_id_type=MESH)

    @pl.when(z < O - 1)
    def _():
        up(img_ref, z).start()

    @pl.when(z > 0)
    def _():
        down(img_ref, z).start()

    for od in range(1, D):
        across(img_ref, od, z).start()
    images[d, z] = img_ref[...]

    shell = shell_ref[...]
    noise = jnp.ones(shell.shape, jnp.float32)
    for i in range(noise_ref.shape[0]):
        noise = jnp.where(shell == i, noise_ref[i], noise)
    w = 1.0 / noise
    w_s[...] = jnp.concatenate([w, w], axis=1)

    def norm_rows(c, carry):
        r0 = pl.multiple_of(c * lanes, lanes)
        x = refs_ref[pl.ds(r0, lanes), :].astype(jnp.float32)
        y = x * x * w_s[...]
        acc = y[:, :128]
        for k in range(1, y.shape[1] // 128):
            acc = acc + y[:, k * 128:(k + 1) * 128]
        rn_s[c] = 0.5 * jnp.sum(acc.T, axis=0, keepdims=True)
        return carry

    lax.fori_loop(0, S, norm_rows, 0)

    def process(src, j):
        scaled = (src[...].astype(jnp.float32) * w_s[...]).astype(jnp.bfloat16)
        full = lax.dot_general(
            scaled, refs_ref[...], (((1,), (1,)), ((), ())), preferred_element_type=jnp.float32)
        for k in range(S):
            part[j, k] = full[:, k * lanes:(k + 1) * lanes] - rn_s[k]
        for o in range(1, S):
            scatter(j, o).start()

    process(img_ref, z)

    def step(t, carry):
        lo = z - t
        hi = z + t

        @pl.when(lo >= 0)
        def _():
            block = images.at[d, lo]
            up(block, lo).wait_recv()

            @pl.when(z < O - 1)
            def _():
                up(block, lo).start()

            for od in range(1, D):
                across(block, od, lo).start()
            process(block, lo)

        @pl.when(hi < O)
        def _():
            block = images.at[d, hi]
            down(block, hi).wait_recv()

            @pl.when(z > 0)
            def _():
                down(block, hi).start()

            for od in range(1, D):
                across(block, od, hi).start()
            process(block, hi)

        return carry

    lax.fori_loop(1, O, step, 0)

    lane = lax.broadcasted_iota(jnp.int32, (img_rows, lanes), 1)

    def reduce_block(j, carry):
        v = part[j, s]
        for o in range(1, S):
            scatter(j, o).wait_recv()
            v = v + recvp[j, o]
        want = jnp.full((img_rows, lanes), j, jnp.int32)
        keep = want == kept_ref[0]
        for k in range(1, most):
            keep = keep | (want == kept_ref[k])
        v = jnp.where(keep, v, floor_value)
        m = jnp.max(v, axis=1, keepdims=True)
        e = jnp.where(keep, jnp.exp(v - m), 0.0)
        total = jnp.sum(e, axis=1, keepdims=True)
        at = pl.ds(pl.multiple_of(j * img_rows, img_rows), img_rows)
        ebuf[at, :] = e.astype(jnp.bfloat16)
        abuf[at, :] = jnp.where(lane == 0, m, total)
        return carry

    lax.fori_loop(0, O, reduce_block, 0)
    lstat[d, s] = abuf[...].T[:2, :]

    def spread(od, os):
        return pltpu.make_async_remote_copy(
            src_ref=lstat.at[d, s], dst_ref=lstat.at[d, s], send_sem=st_send.at[od, os],
            recv_sem=st_recv.at[od, os],
            device_id=dev(z, lax.rem(d + od, D), lax.rem(s + os, S)), device_id_type=MESH)

    peers = [(od, os) for od in range(D) for os in range(S) if od or os]
    for od, os in peers:
        spread(od, os).start()

    def give(to):
        return pltpu.make_async_remote_copy(
            src_ref=ebuf, dst_ref=erecv.at[d, slot], send_sem=e_send.at[to],
            recv_sem=e_recv.at[d, slot], device_id=dev(z, owner, to), device_id_type=MESH)

    def each_give(act):
        for to in range(S):
            @pl.when((owner != d) | (s != to))
            def _():
                act(give(to))

    each_give(lambda c: c.start())

    @pl.when(owner == d)
    def _():
        erecv[d, slot] = ebuf[...]

    for od, os in peers:
        spread(od, os).wait_recv()
    for b in range(D):
        m = lstat[b, 0, 0:1, :]
        for k in range(1, S):
            m = jnp.maximum(m, lstat[b, k, 0:1, :])
        total = jnp.zeros_like(m)
        for k in range(S):
            total = total + lstat[b, k, 1:2, :] * jnp.exp(lstat[b, k, 0:1, :] - m)
        zstat[z, b, 0:1, :] = m
        zstat[z, b, 1:2, :] = total

    def column(o):
        return pltpu.make_async_remote_copy(
            src_ref=zstat.at[z], dst_ref=zstat.at[z], send_sem=z_send.at[o], recv_sem=z_recv.at[o],
            device_id=dev(lax.rem(z + o, O), d, s), device_id_type=MESH)

    for o in range(1, O):
        column(o).start()
    for o in range(1, O):
        column(o).wait_recv()
    for b in range(D):
        m = zstat[0, b, 0:1, :]
        for k in range(1, O):
            m = jnp.maximum(m, zstat[k, b, 0:1, :])
        total = jnp.zeros_like(m)
        for k in range(O):
            total = total + zstat[k, b, 1:2, :] * jnp.exp(zstat[k, b, 0:1, :] - m)
        logn_ref[b:b + 1, :] = m + jnp.log(total)

    def dom_wait(j, carry):
        for od in range(1, D):
            across(images.at[d, j], od, j).wait_recv()
        return carry

    lax.fori_loop(0, O, dom_wait, 0)

    for q in range(per):
        for b in range(D):
            @pl.when((d * per + q != s) | (d != b))
            def _():
                pltpu.make_async_remote_copy(
                    src_ref=ebuf, dst_ref=erecv.at[b, q], send_sem=e_send.at[0],
                    recv_sem=e_recv.at[b, q], device_id=dev(z, lax.rem(d + 1, D), s),
                    device_id_type=MESH).wait_recv()

    depth = O * img_rows
    wide = 512
    probs = []
    for q in range(per):
        line = []
        for b in range(D):
            scale = jnp.exp(lstat[b, d * per + q, 0:1, :] - logn_ref[b:b + 1, :])
            line.append((erecv[b, q].astype(jnp.float32).T * scale).astype(jnp.bfloat16))
        probs.append(jnp.concatenate(line, axis=1))
    for q in range(per):
        erecv_rows = probs[q]
        for c in range(out_ref.shape[1] // wide):
            rhs = images[:, :, :, c * wide:(c + 1) * wide].reshape(D * depth, wide)
            out_ref[q * lanes:(q + 1) * lanes, c * wide:(c + 1) * wide] = jnp.dot(
                erecv_rows, rhs, preferred_element_type=jnp.float32)

    @pl.when(z < O - 1)
    def _():
        def done(j, carry):
            @pl.when(j <= z)
            def _():
                up(img_ref, j).wait_send()
            return carry
        lax.fori_loop(0, O, done, 0)

    @pl.when(z > 0)
    def _():
        def done(j, carry):
            @pl.when(j >= z)
            def _():
                down(img_ref, j).wait_send()
            return carry
        lax.fori_loop(0, O, done, 0)

    def sent(j, carry):
        for od in range(1, D):
            across(img_ref, od, j).wait_send()
        for o in range(1, S):
            scatter(j, o).wait_send()
        return carry

    lax.fori_loop(0, O, sent, 0)
    for od, os in peers:
        spread(od, os).wait_send()
    each_give(lambda c: c.wait_send())
    for o in range(1, O):
        column(o).wait_send()


def shards(references, images, noise_var, shell_of, kept_blocks):
    O, D, S = (lax.axis_size(a) for a in ("orient", "dom", "shell"))
    rows = references.shape[0]
    img_rows = images.shape[0]
    local = references.shape[2]
    flat = 2 * local
    lanes = rows // S
    own = rows // D
    columns = O * img_rows
    vmem = pl.BlockSpec(memory_space=pltpu.VMEM)
    smem = pl.BlockSpec(memory_space=pltpu.SMEM)
    sem = pltpu.SemaphoreType.DMA
    f32, bf16 = jnp.float32, jnp.bfloat16
    out, logn = pl.pallas_call(
        functools.partial(kernel, (O, D, S)),
        name="expectation",
        out_shape=(jax.ShapeDtypeStruct((own, flat), f32), jax.ShapeDtypeStruct((D, columns), f32)),
        in_specs=[smem, smem, vmem, vmem, vmem],
        out_specs=(vmem, vmem),
        scratch_shapes=[
            pltpu.VMEM((D, O, img_rows, flat), bf16),
            pltpu.VMEM((O, S, img_rows, lanes), f32),
            pltpu.VMEM((O, S, img_rows, lanes), f32),
            pltpu.VMEM((columns, lanes), bf16),
            pltpu.VMEM((columns, lanes), f32),
            pltpu.VMEM((D, S // D, columns, lanes), bf16),
            pltpu.VMEM((D, S, 2, columns), f32),
            pltpu.VMEM((O, D, 2, columns), f32),
            pltpu.VMEM((1, flat), f32),
            pltpu.VMEM((S, 1, lanes), f32),
            sem((O,)), sem((O,)), sem((O,)),
            sem((D, O)), sem((D, O)),
            sem((O, S)), sem((O, S)),
            sem((D, S)), sem((D, S)),
            sem((S,)), sem((D, S // D)),
            sem((O,)), sem((O,)),
        ],
        compiler_params=pltpu.CompilerParams(collective_id=0, has_side_effects=True),
    )(
        kept_blocks.reshape(-1),
        noise_var,
        shell_of.reshape(1, -1),
        references.reshape(rows, flat),
        images.reshape(img_rows, flat),
    )
    log_norm = lax.dynamic_slice(
        logn, (lax.axis_index("dom"), lax.axis_index("orient") * img_rows), (1, img_rows))
    return out.reshape(own, 2, local), log_norm.reshape(img_rows)


def solution(mesh):
    placed = (
        P("orient", None, "shell"),
        P(("orient", "dom"), None, "shell"),
        P(),
        P("shell"),
        P("orient", "dom", None),
    )
    return jax.shard_map(
        shards,
        mesh=mesh,
        in_specs=placed,
        out_specs=(P(("orient", "dom"), None, "shell"), P(("orient", "dom"))),
        check_vma=False,
    )
```

```python
import functools

import jax
import jax.numpy as jnp
from jax import lax
from jax.experimental import pallas as pl
from jax.experimental.pallas import tpu as pltpu
from jax.sharding import PartitionSpec as P

floor_value = -1e30
MESH = pl.DeviceIdType.MESH


def kernel(
    sizes, kept_ref, noise_ref, shell_ref, refs_ref, img_ref, prob_ref, home_ref, keep_ref,
    images, part, accum, logn_ref, recvp, ebuf, abuf, erecv, lstat, zstat, w_s, rn_s,
    up_sem, dn_sem, img_sem, dom_send, dom_recv, rs_send, rs_recv,
    st_send, st_recv, e_send, e_recv, z_send, z_recv, out_sem,
):
    O, D, S = sizes
    z, d, s = lax.axis_index("orient"), lax.axis_index("dom"), lax.axis_index("shell")
    rows = refs_ref.shape[0]
    img_rows = img_ref.shape[1]
    half = img_ref.shape[2]
    lanes = rows // S
    per = S // D
    most = kept_ref.shape[0]
    owner = s // per
    slot = s % per

    def dev(a, b, c):
        return {"orient": a, "dom": b, "shell": c}

    barrier = pltpu.get_barrier_semaphore()
    for o in range(1, O):
        pl.semaphore_signal(barrier, inc=1, device_id=dev(lax.rem(z + o, O), d, s), device_id_type=MESH)
    for od in range(D):
        for os in range(S):
            if od or os:
                pl.semaphore_signal(
                    barrier, inc=1,
                    device_id=dev(z, lax.rem(d + od, D), lax.rem(s + os, S)),
                    device_id_type=MESH,
                )
    pl.semaphore_wait(barrier, O - 1 + D * S - 1)

    def up(src, j, c):
        return pltpu.make_async_remote_copy(
            src_ref=src.at[c], dst_ref=images.at[d, j, c], send_sem=up_sem.at[j, c],
            recv_sem=img_sem.at[j, c],
            device_id=dev(lax.rem(z + 1, O), d, s), device_id_type=MESH)

    def down(src, j, c):
        return pltpu.make_async_remote_copy(
            src_ref=src.at[c], dst_ref=images.at[d, j, c], send_sem=dn_sem.at[j, c],
            recv_sem=img_sem.at[j, c],
            device_id=dev(lax.rem(z + O - 1, O), d, s), device_id_type=MESH)

    def across(src, od, j, c):
        return pltpu.make_async_remote_copy(
            src_ref=src.at[c], dst_ref=images.at[d, j, c], send_sem=dom_send.at[od, j, c],
            recv_sem=dom_recv.at[od, j, c],
            device_id=dev(z, lax.rem(d + od, D), s), device_id_type=MESH)

    def scatter(j, o):
        to = lax.rem(s + o, S)
        return pltpu.make_async_remote_copy(
            src_ref=part.at[j, to], dst_ref=recvp.at[j, o], send_sem=rs_send.at[j, o],
            recv_sem=rs_recv.at[j, o], device_id=dev(z, d, to), device_id_type=MESH)

    @pl.when(z < O - 1)
    def _():
        for c in range(2):
            up(img_ref, z, c).start()

    @pl.when(z > 0)
    def _():
        for c in range(2):
            down(img_ref, z, c).start()

    for od in range(1, D):
        for c in range(2):
            across(img_ref, od, z, c).start()

    def keep_copy(src, b, j, c):
        return pltpu.make_async_copy(src.at[c], keep_ref.at[c, b, j], out_sem.at[b, j, c])

    for c in range(2):
        keep_copy(img_ref, d, z, c).start()

    shell = shell_ref[...]
    noise = jnp.ones(shell.shape, jnp.float32)
    for i in range(noise_ref.shape[0]):
        noise = jnp.where(shell == i, noise_ref[i], noise)
    w = 1.0 / noise
    w_s[...] = w

    def norm_rows(c, carry):
        r0 = pl.multiple_of(c * lanes, lanes)
        x0 = refs_ref[pl.ds(r0, lanes), :half].astype(jnp.float32)
        x1 = refs_ref[pl.ds(r0, lanes), half:].astype(jnp.float32)
        y = (x0 * x0 + x1 * x1) * w_s[...]
        acc = y[:, :128]
        for k in range(1, y.shape[1] // 128):
            acc = acc + y[:, k * 128:(k + 1) * 128]
        rn_s[c] = 0.5 * jnp.sum(acc.T, axis=0, keepdims=True)
        return carry

    lax.fori_loop(0, S, norm_rows, 0)

    def cross(src, c):
        scaled = (src[c].astype(jnp.float32) * w_s[...]).astype(jnp.bfloat16)
        return lax.dot_general(
            scaled, refs_ref[:, c * half:(c + 1) * half], (((1,), (1,)), ((), ())),
            preferred_element_type=jnp.float32)

    def finish(full, j):
        for k in range(S):
            part[j, k] = full[:, k * lanes:(k + 1) * lanes] - rn_s[k]
        for o in range(1, S):
            scatter(j, o).start()

    finish(cross(img_ref, 0) + cross(img_ref, 1), z)

    def arrive(block, j, c, hop, onward):
        hop(block, j, c).wait_recv()

        @pl.when(onward)
        def _():
            hop(block, j, c).start()

        for od in range(1, D):
            across(block, od, j, c).start()
        keep_copy(block, d, j, c).start()

    def step(t, carry):
        lo = z - t
        hi = z + t
        for c in range(2):
            @pl.when(lo >= 0)
            def _():
                arrive(images.at[d, lo], lo, c, up, z < O - 1)

            @pl.when(hi < O)
            def _():
                arrive(images.at[d, hi], hi, c, down, z > 0)

            for side, j, ok in ((0, lo, lo >= 0), (1, hi, hi < O)):
                @pl.when(ok)
                def _():
                    full = cross(images.at[d, j], c)
                    if c == 0:
                        accum[side] = full
                    else:
                        finish(accum[side] + full, j)

        return carry

    lax.fori_loop(1, O, step, 0)

    lane = lax.broadcasted_iota(jnp.int32, (img_rows, lanes), 1)

    def reduce_block(j, carry):
        v = part[j, s]
        for o in range(1, S):
            scatter(j, o).wait_recv()
            v = v + recvp[j, o]
        want = jnp.full((img_rows, lanes), j, jnp.int32)
        keep = want == kept_ref[0]
        for k in range(1, most):
            keep = keep | (want == kept_ref[k])
        v = jnp.where(keep, v, floor_value)
        m = jnp.max(v, axis=1, keepdims=True)
        e = jnp.where(keep, jnp.exp(v - m), 0.0)
        total = jnp.sum(e, axis=1, keepdims=True)
        at = pl.ds(pl.multiple_of(j * img_rows, img_rows), img_rows)
        ebuf[at, :] = e.astype(jnp.bfloat16)
        abuf[at, :] = jnp.where(lane == 0, m, total)
        return carry

    lax.fori_loop(0, O, reduce_block, 0)
    lstat[d, s] = abuf[...].T[:2, :]

    def spread(od, os):
        return pltpu.make_async_remote_copy(
            src_ref=lstat.at[d, s], dst_ref=lstat.at[d, s], send_sem=st_send.at[od, os],
            recv_sem=st_recv.at[od, os],
            device_id=dev(z, lax.rem(d + od, D), lax.rem(s + os, S)), device_id_type=MESH)

    peers = [(od, os) for od in range(D) for os in range(S) if od or os]
    for od, os in peers:
        spread(od, os).start()

    def give(to):
        return pltpu.make_async_remote_copy(
            src_ref=ebuf, dst_ref=erecv.at[d, slot], send_sem=e_send.at[to],
            recv_sem=e_recv.at[d, slot], device_id=dev(z, owner, to), device_id_type=MESH)

    def each_give(act):
        for to in range(S):
            @pl.when((owner != d) | (s != to))
            def _():
                act(give(to))

    each_give(lambda c: c.start())

    @pl.when(owner == d)
    def _():
        erecv[d, slot] = ebuf[...]

    for od, os in peers:
        spread(od, os).wait_recv()
    for b in range(D):
        m = lstat[b, 0, 0:1, :]
        for k in range(1, S):
            m = jnp.maximum(m, lstat[b, k, 0:1, :])
        total = jnp.zeros_like(m)
        for k in range(S):
            total = total + lstat[b, k, 1:2, :] * jnp.exp(lstat[b, k, 0:1, :] - m)
        zstat[z, b, 0:1, :] = m
        zstat[z, b, 1:2, :] = total

    def column(o):
        return pltpu.make_async_remote_copy(
            src_ref=zstat.at[z], dst_ref=zstat.at[z], send_sem=z_send.at[o], recv_sem=z_recv.at[o],
            device_id=dev(lax.rem(z + o, O), d, s), device_id_type=MESH)

    for o in range(1, O):
        column(o).start()
    for o in range(1, O):
        column(o).wait_recv()
    for b in range(D):
        m = zstat[0, b, 0:1, :]
        for k in range(1, O):
            m = jnp.maximum(m, zstat[k, b, 0:1, :])
        total = jnp.zeros_like(m)
        for k in range(O):
            total = total + zstat[k, b, 1:2, :] * jnp.exp(zstat[k, b, 0:1, :] - m)
        logn_ref[b:b + 1, :] = m + jnp.log(total)

    home = logn_ref[pl.ds(d, 1), :]
    pick = home[:, :img_rows]
    for j in range(1, O):
        pick = jnp.where(z == j, home[:, j * img_rows:(j + 1) * img_rows], pick)
    home_ref[...] = pick

    def dom_wait(j, carry):
        for od in range(1, D):
            b = lax.rem(d + D - od, D)
            for c in range(2):
                across(images.at[d, j], od, j, c).wait_recv()
                keep_copy(images.at[b, j], b, j, c).start()
        return carry

    lax.fori_loop(0, O, dom_wait, 0)

    for q in range(per):
        for b in range(D):
            @pl.when((d * per + q != s) | (d != b))
            def _():
                pltpu.make_async_remote_copy(
                    src_ref=ebuf, dst_ref=erecv.at[b, q], send_sem=e_send.at[0],
                    recv_sem=e_recv.at[b, q], device_id=dev(z, lax.rem(d + 1, D), s),
                    device_id_type=MESH).wait_recv()

    depth = O * img_rows
    for q in range(per):
        for b in range(D):
            scale = jnp.exp(lstat[b, d * per + q, 0:1, :] - logn_ref[b:b + 1, :])
            p = (erecv[b, q].astype(jnp.float32).T * scale).astype(jnp.bfloat16)
            prob_ref[q * lanes:(q + 1) * lanes, b * depth:(b + 1) * depth] = p

    @pl.when(z < O - 1)
    def _():
        def done(j, carry):
            @pl.when(j <= z)
            def _():
                for c in range(2):
                    up(img_ref, j, c).wait_send()
            return carry
        lax.fori_loop(0, O, done, 0)

    @pl.when(z > 0)
    def _():
        def done(j, carry):
            @pl.when(j >= z)
            def _():
                for c in range(2):
                    down(img_ref, j, c).wait_send()
            return carry
        lax.fori_loop(0, O, done, 0)

    def sent(j, carry):
        for od in range(1, D):
            for c in range(2):
                across(img_ref, od, j, c).wait_send()
        for b in range(D):
            for c in range(2):
                keep_copy(img_ref, b, j, c).wait()
        for o in range(1, S):
            scatter(j, o).wait_send()
        return carry

    lax.fori_loop(0, O, sent, 0)
    for od, os in peers:
        spread(od, os).wait_send()
    each_give(lambda c: c.wait_send())
    for o in range(1, O):
        column(o).wait_send()


def product(prob_ref, home_ref, keep_ref, out_ref, logn_ref, images, total, in_sem, out_sem):
    halves, width, wide = 2, images.shape[2], 512

    def fetch(c):
        return pltpu.make_async_copy(keep_ref.at[c], images.at[c], in_sem.at[c])

    def put(c, n):
        cols = pl.ds(n * wide, wide)
        return pltpu.make_async_copy(
            total.at[c, :, cols], out_ref.at[:, c, cols], out_sem.at[c, n])

    for c in range(halves):
        fetch(c).start()
    logn_ref[...] = home_ref[...]
    for c in range(halves):
        fetch(c).wait()
        for n in range(width // wide):
            cols = slice(n * wide, (n + 1) * wide)
            total[c, :, cols] = jnp.dot(
                prob_ref[...], images[c, :, cols], preferred_element_type=jnp.float32)
            put(c, n).start()
    for c in range(halves):
        for n in range(width // wide):
            put(c, n).wait()


def shards(references, images, noise_var, shell_of, kept_blocks):
    O, D, S = (lax.axis_size(a) for a in ("orient", "dom", "shell"))
    rows = references.shape[0]
    img_rows = images.shape[0]
    local = references.shape[2]
    flat = 2 * local
    lanes = rows // S
    own = rows // D
    columns = O * img_rows
    vmem = pl.BlockSpec(memory_space=pltpu.VMEM)
    smem = pl.BlockSpec(memory_space=pltpu.SMEM)
    sem = pltpu.SemaphoreType.DMA
    f32, bf16 = jnp.float32, jnp.bfloat16
    probs, home, kept_images = pl.pallas_call(
        functools.partial(kernel, (O, D, S)),
        name="expectation",
        out_shape=(
            jax.ShapeDtypeStruct((own, D * columns), bf16),
            jax.ShapeDtypeStruct((1, img_rows), f32),
            jax.ShapeDtypeStruct((2, D, O, img_rows, local), bf16),
        ),
        in_specs=[smem, smem, vmem, vmem, vmem],
        out_specs=(vmem, vmem, pl.BlockSpec(memory_space=pl.ANY)),
        scratch_shapes=[
            pltpu.VMEM((D, O, 2, img_rows, local), bf16),
            pltpu.VMEM((O, S, img_rows, lanes), f32),
            pltpu.VMEM((2, img_rows, rows), f32),
            pltpu.VMEM((D, columns), f32),
            pltpu.VMEM((O, S, img_rows, lanes), f32),
            pltpu.VMEM((columns, lanes), bf16),
            pltpu.VMEM((columns, lanes), f32),
            pltpu.VMEM((D, S // D, columns, lanes), bf16),
            pltpu.VMEM((D, S, 2, columns), f32),
            pltpu.VMEM((O, D, 2, columns), f32),
            pltpu.VMEM((1, local), f32),
            pltpu.VMEM((S, 1, lanes), f32),
            sem((O, 2)), sem((O, 2)), sem((O, 2)),
            sem((D, O, 2)), sem((D, O, 2)),
            sem((O, S)), sem((O, S)),
            sem((D, S)), sem((D, S)),
            sem((S,)), sem((D, S // D)),
            sem((O,)), sem((O,)), sem((D, O, 2)),
        ],
        compiler_params=pltpu.CompilerParams(collective_id=0, has_side_effects=True),
    )(
        kept_blocks.reshape(-1),
        noise_var,
        shell_of.reshape(1, -1),
        references.reshape(rows, flat),
        jnp.transpose(images, (1, 0, 2)),
    )
    depth = D * columns
    weighted, log_norm = pl.pallas_call(
        product,
        name="product",
        out_shape=(
            jax.ShapeDtypeStruct((own, 2, local), f32),
            jax.ShapeDtypeStruct((1, img_rows), f32),
        ),
        in_specs=[vmem, vmem, pl.BlockSpec(memory_space=pl.ANY)],
        out_specs=(pl.BlockSpec(memory_space=pl.ANY), vmem),
        scratch_shapes=[
            pltpu.VMEM((2, depth, local), bf16),
            pltpu.VMEM((2, own, local), f32),
            sem((2,)),
            sem((2, local // 512)),
        ],
    )(probs, home, kept_images.reshape(2, depth, local))
    return weighted, log_norm.reshape(img_rows)


def solution(mesh):
    placed = (
        P("orient", None, "shell"),
        P(("orient", "dom"), None, "shell"),
        P(),
        P("shell"),
        P("orient", "dom", None),
    )
    return jax.shard_map(
        shards,
        mesh=mesh,
        in_specs=placed,
        out_specs=(P(("orient", "dom"), None, "shell"), P(("orient", "dom"))),
        check_vma=False,
    )
```

```python
import functools

import jax
import jax.numpy as jnp
from jax import lax
from jax.experimental import pallas as pl
from jax.experimental.pallas import tpu as pltpu
from jax.sharding import PartitionSpec as P

floor_value = -1e30
MESH = pl.DeviceIdType.MESH


def kernel(
    sizes, kept_ref, noise_ref, shell_ref, raw_ref, flat_ref, prob_ref, home_ref, keep_ref,
    images, part, accum, logn_ref, refs_ref, turned, stage, recvp, ebuf, abuf, erecv, lstat, zstat, w_s, rn_s,
    up_sem, dn_sem, img_sem, dom_send, dom_recv, rs_send, rs_recv,
    st_send, st_recv, e_send, e_recv, z_send, z_recv, out_sem, raw_sem,
):
    O, D, S = sizes
    z, d, s = lax.axis_index("orient"), lax.axis_index("dom"), lax.axis_index("shell")
    rows, _, half = raw_ref.shape
    img_rows = flat_ref.shape[0]
    lanes = rows // S
    per = S // D
    most = kept_ref.shape[0]
    owner = s // per
    slot = s % per

    def dev(a, b, c):
        return {"orient": a, "dom": b, "shell": c}

    barrier = pltpu.get_barrier_semaphore()
    for o in range(1, O):
        pl.semaphore_signal(barrier, inc=1, device_id=dev(lax.rem(z + o, O), d, s), device_id_type=MESH)
    for od in range(D):
        for os in range(S):
            if od or os:
                pl.semaphore_signal(
                    barrier, inc=1,
                    device_id=dev(z, lax.rem(d + od, D), lax.rem(s + os, S)),
                    device_id_type=MESH,
                )
    fetch = pltpu.make_async_copy(raw_ref, stage, raw_sem)
    fetch.start()
    def img_ref(c):
        return flat_ref.at[:, c * half:(c + 1) * half]

    pl.semaphore_wait(barrier, O - 1 + D * S - 1)

    def halves(b, j):
        return lambda c: images.at[b, j, c]

    def up(src, j, c):
        return pltpu.make_async_remote_copy(
            src_ref=src(c), dst_ref=images.at[d, j, c], send_sem=up_sem.at[j, c],
            recv_sem=img_sem.at[j, c],
            device_id=dev(lax.rem(z + 1, O), d, s), device_id_type=MESH)

    def down(src, j, c):
        return pltpu.make_async_remote_copy(
            src_ref=src(c), dst_ref=images.at[d, j, c], send_sem=dn_sem.at[j, c],
            recv_sem=img_sem.at[j, c],
            device_id=dev(lax.rem(z + O - 1, O), d, s), device_id_type=MESH)

    def across(src, od, j, c):
        return pltpu.make_async_remote_copy(
            src_ref=src(c), dst_ref=images.at[d, j, c], send_sem=dom_send.at[od, j, c],
            recv_sem=dom_recv.at[od, j, c],
            device_id=dev(z, lax.rem(d + od, D), s), device_id_type=MESH)

    def scatter(j, o):
        to = lax.rem(s + o, S)
        return pltpu.make_async_remote_copy(
            src_ref=part.at[j, to], dst_ref=recvp.at[j, o], send_sem=rs_send.at[j, o],
            recv_sem=rs_recv.at[j, o], device_id=dev(z, d, to), device_id_type=MESH)

    @pl.when(z < O - 1)
    def _():
        for c in range(2):
            up(img_ref, z, c).start()

    @pl.when(z > 0)
    def _():
        for c in range(2):
            down(img_ref, z, c).start()

    for od in range(1, D):
        for c in range(2):
            across(img_ref, od, z, c).start()

    def keep_copy(src, b, j, c):
        return pltpu.make_async_copy(src(c), keep_ref.at[c, b, j], out_sem.at[b, j, c])

    for c in range(2):
        keep_copy(img_ref, d, z, c).start()

    shell = shell_ref[...]
    noise = jnp.ones(shell.shape, jnp.float32)
    for i in range(noise_ref.shape[0]):
        noise = jnp.where(shell == i, noise_ref[i], noise)
    w = 1.0 / noise
    w_s[...] = w

    def norm_rows(c, carry):
        r0 = pl.multiple_of(c * lanes, lanes)
        x = stage[pl.ds(r0, lanes)]
        refs_ref[pl.ds(r0, lanes), :half] = x[:, 0, :]
        refs_ref[pl.ds(r0, lanes), half:] = x[:, 1, :]
        x0 = refs_ref[pl.ds(r0, lanes), :half].astype(jnp.float32)
        x1 = refs_ref[pl.ds(r0, lanes), half:].astype(jnp.float32)
        y = (x0 * x0 + x1 * x1) * w_s[...]
        acc = y[:, :128]
        for k in range(1, y.shape[1] // 128):
            acc = acc + y[:, k * 128:(k + 1) * 128]
        rn_s[c] = 0.5 * jnp.sum(acc.T, axis=0, keepdims=True)
        return carry

    fetch.wait()
    lax.fori_loop(0, S, norm_rows, 0)

    def cross(src, c):
        scaled = (src(c)[...].astype(jnp.float32) * w_s[...]).astype(jnp.bfloat16)
        return lax.dot_general(
            scaled, refs_ref[:, c * half:(c + 1) * half], (((1,), (1,)), ((), ())),
            preferred_element_type=jnp.float32)

    def finish(full, j):
        for k in range(S):
            part[j, k] = full[:, k * lanes:(k + 1) * lanes] - rn_s[k]
        for o in range(1, S):
            scatter(j, o).start()

    finish(cross(img_ref, 0) + cross(img_ref, 1), z)

    def arrive(block, j, c, hop, onward):
        hop(block, j, c).wait_recv()

        @pl.when(onward)
        def _():
            hop(block, j, c).start()

        for od in range(1, D):
            across(block, od, j, c).start()
        keep_copy(block, d, j, c).start()

    lane = lax.broadcasted_iota(jnp.int32, (img_rows, lanes), 1)

    def reduce_block(j):
        v = part[j, s]
        for o in range(1, S):
            scatter(j, o).wait_recv()
            v = v + recvp[j, o]
        want = jnp.full((img_rows, lanes), j, jnp.int32)
        keep = want == kept_ref[0]
        for k in range(1, most):
            keep = keep | (want == kept_ref[k])
        v = jnp.where(keep, v, floor_value)
        m = jnp.max(v, axis=1, keepdims=True)
        e = jnp.where(keep, jnp.exp(v - m), 0.0)
        total = jnp.sum(e, axis=1, keepdims=True)
        at = pl.ds(pl.multiple_of(j * img_rows, img_rows), img_rows)
        ebuf[at, :] = e.astype(jnp.bfloat16)
        abuf[at, :] = jnp.where(lane == 0, m, total)

    def step(t, carry):
        lo = z - t
        hi = z + t
        for c in range(2):
            @pl.when(lo >= 0)
            def _():
                arrive(halves(d, lo), lo, c, up, z < O - 1)

            @pl.when(hi < O)
            def _():
                arrive(halves(d, hi), hi, c, down, z > 0)

            for side, j, ok in ((0, lo, lo >= 0), (1, hi, hi < O)):
                @pl.when(ok)
                def _():
                    full = cross(halves(d, j), c)
                    if c == 0:
                        accum[side] = full
                    else:
                        finish(accum[side] + full, j)

            if c == 0:
                @pl.when(lo + 1 >= 0)
                def _():
                    reduce_block(lo + 1)

                @pl.when((hi - 1 < O) & (t > 1))
                def _():
                    reduce_block(hi - 1)

        return carry

    lax.fori_loop(1, O, step, 0)

    @pl.when(z == O - 1)
    def _():
        reduce_block(0)

    @pl.when(z == 0)
    def _():
        reduce_block(O - 1)


    lstat[d, s] = abuf[...].T[:2, :]

    def spread(od, os):
        return pltpu.make_async_remote_copy(
            src_ref=lstat.at[d, s], dst_ref=lstat.at[d, s], send_sem=st_send.at[od, os],
            recv_sem=st_recv.at[od, os],
            device_id=dev(z, lax.rem(d + od, D), lax.rem(s + os, S)), device_id_type=MESH)

    peers = [(od, os) for od in range(D) for os in range(S) if od or os]
    for od, os in peers:
        spread(od, os).start()

    def give(to):
        return pltpu.make_async_remote_copy(
            src_ref=ebuf, dst_ref=erecv.at[d, slot], send_sem=e_send.at[to],
            recv_sem=e_recv.at[d, slot], device_id=dev(z, owner, to), device_id_type=MESH)

    def each_give(act):
        for to in range(S):
            @pl.when((owner != d) | (s != to))
            def _():
                act(give(to))

    each_give(lambda c: c.start())

    @pl.when(owner == d)
    def _():
        erecv[d, slot] = ebuf[...]

    for od, os in peers:
        spread(od, os).wait_recv()
    for b in range(D):
        m = lstat[b, 0, 0:1, :]
        for k in range(1, S):
            m = jnp.maximum(m, lstat[b, k, 0:1, :])
        total = jnp.zeros_like(m)
        for k in range(S):
            total = total + lstat[b, k, 1:2, :] * jnp.exp(lstat[b, k, 0:1, :] - m)
        zstat[z, b, 0:1, :] = m
        zstat[z, b, 1:2, :] = total

    def column(o):
        return pltpu.make_async_remote_copy(
            src_ref=zstat.at[z], dst_ref=zstat.at[z], send_sem=z_send.at[o], recv_sem=z_recv.at[o],
            device_id=dev(lax.rem(z + o, O), d, s), device_id_type=MESH)

    for o in range(1, O):
        column(o).start()
    def dom_wait(j, carry):
        for od in range(1, D):
            b = lax.rem(d + D - od, D)
            for c in range(2):
                across(halves(d, j), od, j, c).wait_recv()
                keep_copy(halves(b, j), b, j, c).start()
        return carry

    lax.fori_loop(0, O, dom_wait, 0)

    for q in range(per):
        for b in range(D):
            @pl.when((d * per + q != s) | (d != b))
            def _():
                pltpu.make_async_remote_copy(
                    src_ref=ebuf, dst_ref=erecv.at[b, q], send_sem=e_send.at[0],
                    recv_sem=e_recv.at[b, q], device_id=dev(z, lax.rem(d + 1, D), s),
                    device_id_type=MESH).wait_recv()
    for q in range(per):
        for b in range(D):
            turned[b, q] = erecv[b, q].astype(jnp.float32).T

    for o in range(1, O):
        column(o).wait_recv()
    for b in range(D):
        m = zstat[0, b, 0:1, :]
        for k in range(1, O):
            m = jnp.maximum(m, zstat[k, b, 0:1, :])
        total = jnp.zeros_like(m)
        for k in range(O):
            total = total + zstat[k, b, 1:2, :] * jnp.exp(zstat[k, b, 0:1, :] - m)
        logn_ref[b:b + 1, :] = m + jnp.log(total)

    home = logn_ref[pl.ds(d, 1), :]
    pick = home[:, :img_rows]
    for j in range(1, O):
        pick = jnp.where(z == j, home[:, j * img_rows:(j + 1) * img_rows], pick)
    home_ref[...] = pick


    depth = O * img_rows
    for q in range(per):
        for b in range(D):
            scale = jnp.exp(lstat[b, d * per + q, 0:1, :] - logn_ref[b:b + 1, :])
            p = (turned[b, q] * scale).astype(jnp.bfloat16)
            prob_ref[q * lanes:(q + 1) * lanes, b * depth:(b + 1) * depth] = p

    @pl.when(z < O - 1)
    def _():
        def done(j, carry):
            @pl.when(j <= z)
            def _():
                for c in range(2):
                    up(img_ref, j, c).wait_send()
            return carry
        lax.fori_loop(0, O, done, 0)

    @pl.when(z > 0)
    def _():
        def done(j, carry):
            @pl.when(j >= z)
            def _():
                for c in range(2):
                    down(img_ref, j, c).wait_send()
            return carry
        lax.fori_loop(0, O, done, 0)

    def sent(j, carry):
        for od in range(1, D):
            for c in range(2):
                across(img_ref, od, j, c).wait_send()
        for b in range(D):
            for c in range(2):
                keep_copy(img_ref, b, j, c).wait()
        for o in range(1, S):
            scatter(j, o).wait_send()
        return carry

    lax.fori_loop(0, O, sent, 0)
    for od, os in peers:
        spread(od, os).wait_send()
    each_give(lambda c: c.wait_send())
    for o in range(1, O):
        column(o).wait_send()


def product(prob_ref, home_ref, keep_ref, out_ref, logn_ref, images, total, in_sem, out_sem):
    halves, width, wide = 2, images.shape[2], 512

    def fetch(c):
        return pltpu.make_async_copy(keep_ref.at[c], images.at[c], in_sem.at[c])

    def put(c, n):
        cols = pl.ds(n * wide, wide)
        return pltpu.make_async_copy(
            total.at[c, :, cols], out_ref.at[:, c, cols], out_sem.at[c, n])

    for c in range(halves):
        fetch(c).start()
    logn_ref[...] = home_ref[...]
    for c in range(halves):
        fetch(c).wait()
        for n in range(width // wide):
            cols = slice(n * wide, (n + 1) * wide)
            total[c, :, cols] = jnp.dot(
                prob_ref[...], images[c, :, cols], preferred_element_type=jnp.float32)
            put(c, n).start()
    for c in range(halves):
        for n in range(width // wide):
            put(c, n).wait()


def shards(references, images, noise_var, shell_of, kept_blocks):
    O, D, S = (lax.axis_size(a) for a in ("orient", "dom", "shell"))
    rows = references.shape[0]
    img_rows = images.shape[0]
    local = references.shape[2]
    flat = 2 * local
    lanes = rows // S
    own = rows // D
    columns = O * img_rows
    vmem = pl.BlockSpec(memory_space=pltpu.VMEM)
    smem = pl.BlockSpec(memory_space=pltpu.SMEM)
    sem = pltpu.SemaphoreType.DMA
    f32, bf16 = jnp.float32, jnp.bfloat16
    probs, home, kept_images = pl.pallas_call(
        functools.partial(kernel, (O, D, S)),
        name="expectation",
        out_shape=(
            jax.ShapeDtypeStruct((own, D * columns), bf16),
            jax.ShapeDtypeStruct((1, img_rows), f32),
            jax.ShapeDtypeStruct((2, D, O, img_rows, local), bf16),
        ),
        in_specs=[smem, smem, vmem, pl.BlockSpec(memory_space=pl.ANY), vmem],
        out_specs=(vmem, vmem, pl.BlockSpec(memory_space=pl.ANY)),
        scratch_shapes=[
            pltpu.VMEM((D, O, 2, img_rows, local), bf16),
            pltpu.VMEM((O, S, img_rows, lanes), f32),
            pltpu.VMEM((2, img_rows, rows), f32),
            pltpu.VMEM((D, columns), f32),
            pltpu.VMEM((rows, flat), bf16),
            pltpu.VMEM((D, S // D, lanes, columns), f32),
            pltpu.VMEM((rows, 2, local), bf16),
            pltpu.VMEM((O, S, img_rows, lanes), f32),
            pltpu.VMEM((columns, lanes), bf16),
            pltpu.VMEM((columns, lanes), f32),
            pltpu.VMEM((D, S // D, columns, lanes), bf16),
            pltpu.VMEM((D, S, 2, columns), f32),
            pltpu.VMEM((O, D, 2, columns), f32),
            pltpu.VMEM((1, local), f32),
            pltpu.VMEM((S, 1, lanes), f32),
            sem((O, 2)), sem((O, 2)), sem((O, 2)),
            sem((D, O, 2)), sem((D, O, 2)),
            sem((O, S)), sem((O, S)),
            sem((D, S)), sem((D, S)),
            sem((S,)), sem((D, S // D)),
            sem((O,)), sem((O,)), sem((D, O, 2)), sem,
        ],
        compiler_params=pltpu.CompilerParams(collective_id=0, has_side_effects=True),
    )(
        kept_blocks.reshape(-1),
        noise_var,
        shell_of.reshape(1, -1),
        references,
        images.reshape(img_rows, flat),
    )
    depth = D * columns
    weighted, log_norm = pl.pallas_call(
        product,
        name="product",
        out_shape=(
            jax.ShapeDtypeStruct((own, 2, local), f32),
            jax.ShapeDtypeStruct((1, img_rows), f32),
        ),
        in_specs=[vmem, vmem, pl.BlockSpec(memory_space=pl.ANY)],
        out_specs=(pl.BlockSpec(memory_space=pl.ANY), vmem),
        scratch_shapes=[
            pltpu.VMEM((2, depth, local), bf16),
            pltpu.VMEM((2, own, local), f32),
            sem((2,)),
            sem((2, local // 512)),
        ],
    )(probs, home, kept_images.reshape(2, depth, local))
    return weighted, log_norm.reshape(img_rows)


def solution(mesh):
    placed = (
        P("orient", None, "shell"),
        P(("orient", "dom"), None, "shell"),
        P(),
        P("shell"),
        P("orient", "dom", None),
    )
    return jax.shard_map(
        shards,
        mesh=mesh,
        in_specs=placed,
        out_specs=(P(("orient", "dom"), None, "shell"), P(("orient", "dom"))),
        check_vma=False,
    )
```

```python
import functools

import jax
import jax.numpy as jnp
from jax import lax
from jax.experimental import pallas as pl
from jax.experimental.pallas import tpu as pltpu
from jax.sharding import PartitionSpec as P

floor_value = -1e30
MESH = pl.DeviceIdType.MESH


def kernel(
    sizes, kept_ref, noise_ref, shell_ref, raw_ref, whole_ref, prob_ref, home_ref, keep_ref,
    images, part, accum, logn_ref, refs_ref, turned, stage, img_stage, flat_ref, recvp, ebuf, abuf, erecv, lstat, zstat, w_s, rn_s,
    up_sem, dn_sem, img_sem, dom_send, dom_recv, rs_send, rs_recv,
    st_send, st_recv, e_send, e_recv, z_send, z_recv, out_sem, raw_sem, own_sem,
):
    O, D, S = sizes
    z, d, s = lax.axis_index("orient"), lax.axis_index("dom"), lax.axis_index("shell")
    rows, _, half = raw_ref.shape
    img_rows = whole_ref.shape[0]
    lanes = rows // S
    per = S // D
    most = kept_ref.shape[0]
    owner = s // per
    slot = s % per

    def dev(a, b, c):
        return {"orient": a, "dom": b, "shell": c}

    own = pltpu.make_async_copy(whole_ref, img_stage, own_sem)
    own.start()
    fetch = pltpu.make_async_copy(raw_ref, stage, raw_sem)
    fetch.start()
    barrier = pltpu.get_barrier_semaphore()
    for o in range(1, O):
        pl.semaphore_signal(barrier, inc=1, device_id=dev(lax.rem(z + o, O), d, s), device_id_type=MESH)
    for od in range(D):
        for os in range(S):
            if od or os:
                pl.semaphore_signal(
                    barrier, inc=1,
                    device_id=dev(z, lax.rem(d + od, D), lax.rem(s + os, S)),
                    device_id_type=MESH,
                )
    own.wait()
    x = img_stage[...]
    for c in range(2):
        flat_ref[:, c * half:(c + 1) * half] = x[:, c, :]

    def img_ref(c):
        return flat_ref.at[:, c * half:(c + 1) * half]

    pl.semaphore_wait(barrier, O - 1 + D * S - 1)

    def halves(b, j):
        return lambda c: images.at[b, j, c]

    def up(src, j, c):
        return pltpu.make_async_remote_copy(
            src_ref=src(c), dst_ref=images.at[d, j, c], send_sem=up_sem.at[j, c],
            recv_sem=img_sem.at[j, c],
            device_id=dev(lax.rem(z + 1, O), d, s), device_id_type=MESH)

    def down(src, j, c):
        return pltpu.make_async_remote_copy(
            src_ref=src(c), dst_ref=images.at[d, j, c], send_sem=dn_sem.at[j, c],
            recv_sem=img_sem.at[j, c],
            device_id=dev(lax.rem(z + O - 1, O), d, s), device_id_type=MESH)

    def across(src, od, j, c):
        return pltpu.make_async_remote_copy(
            src_ref=src(c), dst_ref=images.at[d, j, c], send_sem=dom_send.at[od, j, c],
            recv_sem=dom_recv.at[od, j, c],
            device_id=dev(z, lax.rem(d + od, D), s), device_id_type=MESH)

    def scatter(j, o):
        to = lax.rem(s + o, S)
        return pltpu.make_async_remote_copy(
            src_ref=part.at[j, to], dst_ref=recvp.at[j, o], send_sem=rs_send.at[j, o],
            recv_sem=rs_recv.at[j, o], device_id=dev(z, d, to), device_id_type=MESH)

    @pl.when(z < O - 1)
    def _():
        for c in range(2):
            up(img_ref, z, c).start()

    @pl.when(z > 0)
    def _():
        for c in range(2):
            down(img_ref, z, c).start()

    for od in range(1, D):
        for c in range(2):
            across(img_ref, od, z, c).start()

    def keep_copy(src, b, j, c):
        return pltpu.make_async_copy(src(c), keep_ref.at[c, b, j], out_sem.at[b, j, c])

    for c in range(2):
        keep_copy(img_ref, d, z, c).start()

    shell = shell_ref[...]
    noise = jnp.ones(shell.shape, jnp.float32)
    for i in range(noise_ref.shape[0]):
        noise = jnp.where(shell == i, noise_ref[i], noise)
    w = 1.0 / noise
    w_s[...] = w

    def norm_rows(c, carry):
        r0 = pl.multiple_of(c * lanes, lanes)
        x = stage[pl.ds(r0, lanes)]
        refs_ref[pl.ds(r0, lanes), :half] = x[:, 0, :]
        refs_ref[pl.ds(r0, lanes), half:] = x[:, 1, :]
        x0 = refs_ref[pl.ds(r0, lanes), :half].astype(jnp.float32)
        x1 = refs_ref[pl.ds(r0, lanes), half:].astype(jnp.float32)
        y = (x0 * x0 + x1 * x1) * w_s[...]
        acc = y[:, :128]
        for k in range(1, y.shape[1] // 128):
            acc = acc + y[:, k * 128:(k + 1) * 128]
        rn_s[c] = 0.5 * jnp.sum(acc.T, axis=0, keepdims=True)
        return carry

    fetch.wait()
    lax.fori_loop(0, S, norm_rows, 0)

    def cross(src, c):
        scaled = (src(c)[...].astype(jnp.float32) * w_s[...]).astype(jnp.bfloat16)
        return lax.dot_general(
            scaled, refs_ref[:, c * half:(c + 1) * half], (((1,), (1,)), ((), ())),
            preferred_element_type=jnp.float32)

    def finish(full, j):
        for k in range(S):
            part[j, k] = full[:, k * lanes:(k + 1) * lanes] - rn_s[k]
        for o in range(1, S):
            scatter(j, o).start()

    finish(cross(img_ref, 0) + cross(img_ref, 1), z)

    def arrive(block, j, c, hop, onward):
        hop(block, j, c).wait_recv()

        @pl.when(onward)
        def _():
            hop(block, j, c).start()

        for od in range(1, D):
            across(block, od, j, c).start()
        keep_copy(block, d, j, c).start()

    lane = lax.broadcasted_iota(jnp.int32, (img_rows, lanes), 1)

    def reduce_block(j):
        v = part[j, s]
        for o in range(1, S):
            scatter(j, o).wait_recv()
            v = v + recvp[j, o]
        want = jnp.full((img_rows, lanes), j, jnp.int32)
        keep = want == kept_ref[0]
        for k in range(1, most):
            keep = keep | (want == kept_ref[k])
        v = jnp.where(keep, v, floor_value)
        m = jnp.max(v, axis=1, keepdims=True)
        e = jnp.where(keep, jnp.exp(v - m), 0.0)
        total = jnp.sum(e, axis=1, keepdims=True)
        at = pl.ds(pl.multiple_of(j * img_rows, img_rows), img_rows)
        ebuf[at, :] = e.astype(jnp.bfloat16)
        abuf[at, :] = jnp.where(lane == 0, m, total)

    def step(t, carry):
        lo = z - t
        hi = z + t
        for c in range(2):
            @pl.when(lo >= 0)
            def _():
                arrive(halves(d, lo), lo, c, up, z < O - 1)

            @pl.when(hi < O)
            def _():
                arrive(halves(d, hi), hi, c, down, z > 0)

            for side, j, ok in ((0, lo, lo >= 0), (1, hi, hi < O)):
                @pl.when(ok)
                def _():
                    full = cross(halves(d, j), c)
                    if c == 0:
                        accum[side] = full
                    else:
                        finish(accum[side] + full, j)

            if c == 1:
                @pl.when(lo + 1 >= 0)
                def _():
                    reduce_block(lo + 1)

                @pl.when((hi - 1 < O) & (t > 1))
                def _():
                    reduce_block(hi - 1)

        return carry

    lax.fori_loop(1, O, step, 0)

    @pl.when(z == O - 1)
    def _():
        reduce_block(0)

    @pl.when(z == 0)
    def _():
        reduce_block(O - 1)


    lstat[d, s] = abuf[...].T[:2, :]

    def spread(od, os):
        return pltpu.make_async_remote_copy(
            src_ref=lstat.at[d, s], dst_ref=lstat.at[d, s], send_sem=st_send.at[od, os],
            recv_sem=st_recv.at[od, os],
            device_id=dev(z, lax.rem(d + od, D), lax.rem(s + os, S)), device_id_type=MESH)

    peers = [(od, os) for od in range(D) for os in range(S) if od or os]
    for od, os in peers:
        spread(od, os).start()

    def give(to):
        return pltpu.make_async_remote_copy(
            src_ref=ebuf, dst_ref=erecv.at[d, slot], send_sem=e_send.at[to],
            recv_sem=e_recv.at[d, slot], device_id=dev(z, owner, to), device_id_type=MESH)

    def each_give(act):
        for to in range(S):
            @pl.when((owner != d) | (s != to))
            def _():
                act(give(to))

    each_give(lambda c: c.start())

    @pl.when(owner == d)
    def _():
        erecv[d, slot] = ebuf[...]

    for od, os in peers:
        spread(od, os).wait_recv()
    for b in range(D):
        m = lstat[b, 0, 0:1, :]
        for k in range(1, S):
            m = jnp.maximum(m, lstat[b, k, 0:1, :])
        total = jnp.zeros_like(m)
        for k in range(S):
            total = total + lstat[b, k, 1:2, :] * jnp.exp(lstat[b, k, 0:1, :] - m)
        zstat[z, b, 0:1, :] = m
        zstat[z, b, 1:2, :] = total

    def column(o):
        return pltpu.make_async_remote_copy(
            src_ref=zstat.at[z], dst_ref=zstat.at[z], send_sem=z_send.at[o], recv_sem=z_recv.at[o],
            device_id=dev(lax.rem(z + o, O), d, s), device_id_type=MESH)

    for o in range(1, O):
        column(o).start()
    def dom_wait(j, carry):
        for od in range(1, D):
            b = lax.rem(d + D - od, D)
            for c in range(2):
                across(halves(d, j), od, j, c).wait_recv()
                keep_copy(halves(b, j), b, j, c).start()
        return carry

    lax.fori_loop(0, O, dom_wait, 0)

    for q in range(per):
        for b in range(D):
            @pl.when((d * per + q != s) | (d != b))
            def _():
                pltpu.make_async_remote_copy(
                    src_ref=ebuf, dst_ref=erecv.at[b, q], send_sem=e_send.at[0],
                    recv_sem=e_recv.at[b, q], device_id=dev(z, lax.rem(d + 1, D), s),
                    device_id_type=MESH).wait_recv()
    for q in range(per):
        for b in range(D):
            turned[b, q] = erecv[b, q].astype(jnp.float32).T

    for o in range(1, O):
        column(o).wait_recv()
    for b in range(D):
        m = zstat[0, b, 0:1, :]
        for k in range(1, O):
            m = jnp.maximum(m, zstat[k, b, 0:1, :])
        total = jnp.zeros_like(m)
        for k in range(O):
            total = total + zstat[k, b, 1:2, :] * jnp.exp(zstat[k, b, 0:1, :] - m)
        logn_ref[b:b + 1, :] = m + jnp.log(total)

    home = logn_ref[pl.ds(d, 1), :]
    pick = home[:, :img_rows]
    for j in range(1, O):
        pick = jnp.where(z == j, home[:, j * img_rows:(j + 1) * img_rows], pick)
    home_ref[...] = pick


    depth = O * img_rows
    for q in range(per):
        for b in range(D):
            scale = jnp.exp(lstat[b, d * per + q, 0:1, :] - logn_ref[b:b + 1, :])
            p = (turned[b, q] * scale).astype(jnp.bfloat16)
            prob_ref[q * lanes:(q + 1) * lanes, b * depth:(b + 1) * depth] = p

    @pl.when(z < O - 1)
    def _():
        def done(j, carry):
            @pl.when(j <= z)
            def _():
                for c in range(2):
                    up(img_ref, j, c).wait_send()
            return carry
        lax.fori_loop(0, O, done, 0)

    @pl.when(z > 0)
    def _():
        def done(j, carry):
            @pl.when(j >= z)
            def _():
                for c in range(2):
                    down(img_ref, j, c).wait_send()
            return carry
        lax.fori_loop(0, O, done, 0)

    def sent(j, carry):
        for od in range(1, D):
            for c in range(2):
                across(img_ref, od, j, c).wait_send()
        for b in range(D):
            for c in range(2):
                keep_copy(img_ref, b, j, c).wait()
        for o in range(1, S):
            scatter(j, o).wait_send()
        return carry

    lax.fori_loop(0, O, sent, 0)
    for od, os in peers:
        spread(od, os).wait_send()
    each_give(lambda c: c.wait_send())
    for o in range(1, O):
        column(o).wait_send()


def product(prob_ref, home_ref, keep_ref, out_ref, logn_ref, images, total, in_sem, out_sem):
    halves, width, wide = 2, images.shape[2], 512

    def fetch(c, n):
        cols = pl.ds(n * wide, wide)
        return pltpu.make_async_copy(
            keep_ref.at[c, :, cols], images.at[c, :, cols], in_sem.at[c, n])

    def put(c, n):
        cols = pl.ds(n * wide, wide)
        return pltpu.make_async_copy(
            total.at[c, :, cols], out_ref.at[:, c, cols], out_sem.at[c, n])

    for c in range(halves):
        for n in range(width // wide):
            fetch(c, n).start()
    logn_ref[...] = home_ref[...]
    for c in range(halves):
        for n in range(width // wide):
            fetch(c, n).wait()
            cols = slice(n * wide, (n + 1) * wide)
            total[c, :, cols] = jnp.dot(
                prob_ref[...], images[c, :, cols], preferred_element_type=jnp.float32)
            put(c, n).start()
    for c in range(halves):
        for n in range(width // wide):
            put(c, n).wait()


def shards(references, images, noise_var, shell_of, kept_blocks):
    O, D, S = (lax.axis_size(a) for a in ("orient", "dom", "shell"))
    rows = references.shape[0]
    img_rows = images.shape[0]
    local = references.shape[2]
    flat = 2 * local
    lanes = rows // S
    own = rows // D
    columns = O * img_rows
    vmem = pl.BlockSpec(memory_space=pltpu.VMEM)
    smem = pl.BlockSpec(memory_space=pltpu.SMEM)
    sem = pltpu.SemaphoreType.DMA
    f32, bf16 = jnp.float32, jnp.bfloat16
    probs, home, kept_images = pl.pallas_call(
        functools.partial(kernel, (O, D, S)),
        name="expectation",
        out_shape=(
            jax.ShapeDtypeStruct((own, D * columns), bf16),
            jax.ShapeDtypeStruct((1, img_rows), f32),
            jax.ShapeDtypeStruct((2, D, O, img_rows, local), bf16),
        ),
        in_specs=[smem, smem, vmem, pl.BlockSpec(memory_space=pl.ANY), pl.BlockSpec(memory_space=pl.ANY)],
        out_specs=(vmem, vmem, pl.BlockSpec(memory_space=pl.ANY)),
        scratch_shapes=[
            pltpu.VMEM((D, O, 2, img_rows, local), bf16),
            pltpu.VMEM((O, S, img_rows, lanes), f32),
            pltpu.VMEM((2, img_rows, rows), f32),
            pltpu.VMEM((D, columns), f32),
            pltpu.VMEM((rows, flat), bf16),
            pltpu.VMEM((D, S // D, lanes, columns), f32),
            pltpu.VMEM((rows, 2, local), bf16),
            pltpu.VMEM((img_rows, 2, local), bf16),
            pltpu.VMEM((img_rows, flat), bf16),
            pltpu.VMEM((O, S, img_rows, lanes), f32),
            pltpu.VMEM((columns, lanes), bf16),
            pltpu.VMEM((columns, lanes), f32),
            pltpu.VMEM((D, S // D, columns, lanes), bf16),
            pltpu.VMEM((D, S, 2, columns), f32),
            pltpu.VMEM((O, D, 2, columns), f32),
            pltpu.VMEM((1, local), f32),
            pltpu.VMEM((S, 1, lanes), f32),
            sem((O, 2)), sem((O, 2)), sem((O, 2)),
            sem((D, O, 2)), sem((D, O, 2)),
            sem((O, S)), sem((O, S)),
            sem((D, S)), sem((D, S)),
            sem((S,)), sem((D, S // D)),
            sem((O,)), sem((O,)), sem((D, O, 2)), sem, sem,
        ],
        compiler_params=pltpu.CompilerParams(collective_id=0, has_side_effects=True),
    )(
        kept_blocks.reshape(-1),
        noise_var,
        shell_of.reshape(1, -1),
        references,
        images,
    )
    depth = D * columns
    weighted, log_norm = pl.pallas_call(
        product,
        name="product",
        out_shape=(
            jax.ShapeDtypeStruct((own, 2, local), f32),
            jax.ShapeDtypeStruct((1, img_rows), f32),
        ),
        in_specs=[vmem, vmem, pl.BlockSpec(memory_space=pl.ANY)],
        out_specs=(pl.BlockSpec(memory_space=pl.ANY), vmem),
        scratch_shapes=[
            pltpu.VMEM((2, depth, local), bf16),
            pltpu.VMEM((2, own, local), f32),
            sem((2, local // 512)),
            sem((2, local // 512)),
        ],
    )(probs, home, kept_images.reshape(2, depth, local))
    return weighted, log_norm.reshape(img_rows)


def solution(mesh):
    placed = (
        P("orient", None, "shell"),
        P(("orient", "dom"), None, "shell"),
        P(),
        P("shell"),
        P("orient", "dom", None),
    )
    return jax.shard_map(
        shards,
        mesh=mesh,
        in_specs=placed,
        out_specs=(P(("orient", "dom"), None, "shell"), P(("orient", "dom"))),
        check_vma=False,
    )
```

```python
import functools

import jax
import jax.numpy as jnp
from jax import lax
from jax.experimental import pallas as pl
from jax.experimental.pallas import tpu as pltpu
from jax.sharding import PartitionSpec as P

floor_value = -1e30
MESH = pl.DeviceIdType.MESH


def kernel(
    sizes, kept_ref, noise_ref, shell_ref, raw_ref, whole_ref, prob_ref, home_ref, keep_ref,
    images, part, accum, logn_ref, refs_ref, turned, stage, img_stage, flat_ref, recvp, ebuf, abuf, erecv, lstat, zstat, w_s, rn_s,
    up_sem, dn_sem, img_sem, dom_send, dom_recv, rs_send, rs_recv,
    st_send, st_recv, e_send, e_recv, z_send, z_recv, out_sem, raw_sem, own_sem,
):
    O, D, S = sizes
    z, d, s = lax.axis_index("orient"), lax.axis_index("dom"), lax.axis_index("shell")
    rows, _, half = raw_ref.shape
    img_rows = whole_ref.shape[0]
    lanes = rows // S
    per = S // D
    most = kept_ref.shape[0]
    owner = s // per
    slot = s % per

    def dev(a, b, c):
        return {"orient": a, "dom": b, "shell": c}

    own = pltpu.make_async_copy(whole_ref, img_stage, own_sem)
    own.start()
    fetch = pltpu.make_async_copy(raw_ref, stage, raw_sem)
    fetch.start()
    barrier = pltpu.get_barrier_semaphore()
    for o in range(1, O):
        pl.semaphore_signal(barrier, inc=1, device_id=dev(lax.rem(z + o, O), d, s), device_id_type=MESH)
    for od in range(D):
        for os in range(S):
            if od or os:
                pl.semaphore_signal(
                    barrier, inc=1,
                    device_id=dev(z, lax.rem(d + od, D), lax.rem(s + os, S)),
                    device_id_type=MESH,
                )
    own.wait()
    x = img_stage[...]
    for c in range(2):
        flat_ref[:, c * half:(c + 1) * half] = x[:, c, :]

    def img_ref(c):
        return flat_ref.at[:, c * half:(c + 1) * half]

    pl.semaphore_wait(barrier, O - 1 + D * S - 1)

    def halves(b, j):
        return lambda c: images.at[b, j, c]

    def up(src, j, c):
        return pltpu.make_async_remote_copy(
            src_ref=src(c), dst_ref=images.at[d, j, c], send_sem=up_sem.at[j, c],
            recv_sem=img_sem.at[j, c],
            device_id=dev(lax.rem(z + 1, O), d, s), device_id_type=MESH)

    def down(src, j, c):
        return pltpu.make_async_remote_copy(
            src_ref=src(c), dst_ref=images.at[d, j, c], send_sem=dn_sem.at[j, c],
            recv_sem=img_sem.at[j, c],
            device_id=dev(lax.rem(z + O - 1, O), d, s), device_id_type=MESH)

    def across(src, od, j, c):
        return pltpu.make_async_remote_copy(
            src_ref=src(c), dst_ref=images.at[d, j, c], send_sem=dom_send.at[od, j, c],
            recv_sem=dom_recv.at[od, j, c],
            device_id=dev(z, lax.rem(d + od, D), s), device_id_type=MESH)

    def scatter(j, o):
        to = lax.rem(s + o, S)
        return pltpu.make_async_remote_copy(
            src_ref=part.at[j, to], dst_ref=recvp.at[j, o], send_sem=rs_send.at[j, o],
            recv_sem=rs_recv.at[j, o], device_id=dev(z, d, to), device_id_type=MESH)

    @pl.when(z < O - 1)
    def _():
        for c in range(2):
            up(img_ref, z, c).start()

    @pl.when(z > 0)
    def _():
        for c in range(2):
            down(img_ref, z, c).start()

    for od in range(1, D):
        for c in range(2):
            across(img_ref, od, z, c).start()

    def keep_copy(src, b, j, c):
        return pltpu.make_async_copy(src(c), keep_ref.at[c, b, j], out_sem.at[b, j, c])

    for c in range(2):
        keep_copy(img_ref, d, z, c).start()

    shell = shell_ref[...]
    noise = jnp.ones(shell.shape, jnp.float32)
    for i in range(noise_ref.shape[0]):
        noise = jnp.where(shell == i, noise_ref[i], noise)
    w = 1.0 / noise
    w_s[...] = w

    def norm_rows(c, carry):
        r0 = pl.multiple_of(c * lanes, lanes)
        x = stage[pl.ds(r0, lanes)]
        refs_ref[pl.ds(r0, lanes), :half] = x[:, 0, :]
        refs_ref[pl.ds(r0, lanes), half:] = x[:, 1, :]
        x0 = refs_ref[pl.ds(r0, lanes), :half].astype(jnp.float32)
        x1 = refs_ref[pl.ds(r0, lanes), half:].astype(jnp.float32)
        y = (x0 * x0 + x1 * x1) * w_s[...]
        acc = y[:, :128]
        for k in range(1, y.shape[1] // 128):
            acc = acc + y[:, k * 128:(k + 1) * 128]
        rn_s[c] = 0.5 * jnp.sum(acc.T, axis=0, keepdims=True)
        return carry

    fetch.wait()
    lax.fori_loop(0, S, norm_rows, 0)

    def cross(src, c):
        scaled = (src(c)[...].astype(jnp.float32) * w_s[...]).astype(jnp.bfloat16)
        return lax.dot_general(
            scaled, refs_ref[:, c * half:(c + 1) * half], (((1,), (1,)), ((), ())),
            preferred_element_type=jnp.float32)

    def finish(full, j):
        for k in range(S):
            part[j, k] = full[:, k * lanes:(k + 1) * lanes] - rn_s[k]
        for o in range(1, S):
            scatter(j, o).start()

    def own_block():
        finish(cross(img_ref, 0) + cross(img_ref, 1), z)

    if O == 1:
        own_block()

    def arrive(block, j, c, hop, onward):
        hop(block, j, c).wait_recv()

        @pl.when(onward)
        def _():
            hop(block, j, c).start()

        for od in range(1, D):
            across(block, od, j, c).start()
        keep_copy(block, d, j, c).start()

    lane = lax.broadcasted_iota(jnp.int32, (img_rows, lanes), 1)

    def reduce_block(j):
        v = part[j, s]
        for o in range(1, S):
            scatter(j, o).wait_recv()
            v = v + recvp[j, o]
        want = jnp.full((img_rows, lanes), j, jnp.int32)
        keep = want == kept_ref[0]
        for k in range(1, most):
            keep = keep | (want == kept_ref[k])
        v = jnp.where(keep, v, floor_value)
        m = jnp.max(v, axis=1, keepdims=True)
        e = jnp.where(keep, jnp.exp(v - m), 0.0)
        total = jnp.sum(e, axis=1, keepdims=True)
        at = pl.ds(pl.multiple_of(j * img_rows, img_rows), img_rows)
        ebuf[at, :] = e.astype(jnp.bfloat16)
        abuf[at, :] = jnp.where(lane == 0, m, total)

    def step(t, carry):
        lo = z - t
        hi = z + t
        for c in range(2):
            @pl.when(lo >= 0)
            def _():
                arrive(halves(d, lo), lo, c, up, z < O - 1)

            @pl.when(hi < O)
            def _():
                arrive(halves(d, hi), hi, c, down, z > 0)

            if c == 0:
                pl.when(t == 1)(own_block)

            for side, j, ok in ((0, lo, lo >= 0), (1, hi, hi < O)):
                @pl.when(ok)
                def _():
                    full = cross(halves(d, j), c)
                    if c == 0:
                        accum[side] = full
                    else:
                        finish(accum[side] + full, j)

            if c == 1:
                @pl.when(lo + 1 >= 0)
                def _():
                    reduce_block(lo + 1)

                @pl.when((hi - 1 < O) & (t > 1))
                def _():
                    reduce_block(hi - 1)

        return carry

    lax.fori_loop(1, O, step, 0)

    @pl.when(z == O - 1)
    def _():
        reduce_block(0)

    @pl.when(z == 0)
    def _():
        reduce_block(O - 1)


    lstat[d, s] = abuf[...].T[:2, :]

    def spread(od, os):
        return pltpu.make_async_remote_copy(
            src_ref=lstat.at[d, s], dst_ref=lstat.at[d, s], send_sem=st_send.at[od, os],
            recv_sem=st_recv.at[od, os],
            device_id=dev(z, lax.rem(d + od, D), lax.rem(s + os, S)), device_id_type=MESH)

    peers = [(od, os) for od in range(D) for os in range(S) if od or os]
    for od, os in peers:
        spread(od, os).start()

    def give(to):
        return pltpu.make_async_remote_copy(
            src_ref=ebuf, dst_ref=erecv.at[d, slot], send_sem=e_send.at[to],
            recv_sem=e_recv.at[d, slot], device_id=dev(z, owner, to), device_id_type=MESH)

    def each_give(act):
        for to in range(S):
            @pl.when((owner != d) | (s != to))
            def _():
                act(give(to))

    each_give(lambda c: c.start())

    @pl.when(owner == d)
    def _():
        erecv[d, slot] = ebuf[...]

    for od, os in peers:
        spread(od, os).wait_recv()
    for b in range(D):
        m = lstat[b, 0, 0:1, :]
        for k in range(1, S):
            m = jnp.maximum(m, lstat[b, k, 0:1, :])
        total = jnp.zeros_like(m)
        for k in range(S):
            total = total + lstat[b, k, 1:2, :] * jnp.exp(lstat[b, k, 0:1, :] - m)
        zstat[z, b, 0:1, :] = m
        zstat[z, b, 1:2, :] = total

    def column(o):
        return pltpu.make_async_remote_copy(
            src_ref=zstat.at[z], dst_ref=zstat.at[z], send_sem=z_send.at[o], recv_sem=z_recv.at[o],
            device_id=dev(lax.rem(z + o, O), d, s), device_id_type=MESH)

    for o in range(1, O):
        column(o).start()
    def dom_wait(j, carry):
        for od in range(1, D):
            b = lax.rem(d + D - od, D)
            for c in range(2):
                across(halves(d, j), od, j, c).wait_recv()
                keep_copy(halves(b, j), b, j, c).start()
        return carry

    lax.fori_loop(0, O, dom_wait, 0)

    for q in range(per):
        for b in range(D):
            @pl.when((d * per + q != s) | (d != b))
            def _():
                pltpu.make_async_remote_copy(
                    src_ref=ebuf, dst_ref=erecv.at[b, q], send_sem=e_send.at[0],
                    recv_sem=e_recv.at[b, q], device_id=dev(z, lax.rem(d + 1, D), s),
                    device_id_type=MESH).wait_recv()
    for q in range(per):
        for b in range(D):
            turned[b, q] = erecv[b, q].astype(jnp.float32).T

    for o in range(1, O):
        column(o).wait_recv()
    for b in range(D):
        m = zstat[0, b, 0:1, :]
        for k in range(1, O):
            m = jnp.maximum(m, zstat[k, b, 0:1, :])
        total = jnp.zeros_like(m)
        for k in range(O):
            total = total + zstat[k, b, 1:2, :] * jnp.exp(zstat[k, b, 0:1, :] - m)
        logn_ref[b:b + 1, :] = m + jnp.log(total)

    home = logn_ref[pl.ds(d, 1), :]
    pick = home[:, :img_rows]
    for j in range(1, O):
        pick = jnp.where(z == j, home[:, j * img_rows:(j + 1) * img_rows], pick)
    home_ref[...] = pick


    depth = O * img_rows
    for q in range(per):
        for b in range(D):
            scale = jnp.exp(lstat[b, d * per + q, 0:1, :] - logn_ref[b:b + 1, :])
            p = (turned[b, q] * scale).astype(jnp.bfloat16)
            prob_ref[q * lanes:(q + 1) * lanes, b * depth:(b + 1) * depth] = p

    @pl.when(z < O - 1)
    def _():
        def done(j, carry):
            @pl.when(j <= z)
            def _():
                for c in range(2):
                    up(img_ref, j, c).wait_send()
            return carry
        lax.fori_loop(0, O, done, 0)

    @pl.when(z > 0)
    def _():
        def done(j, carry):
            @pl.when(j >= z)
            def _():
                for c in range(2):
                    down(img_ref, j, c).wait_send()
            return carry
        lax.fori_loop(0, O, done, 0)

    def sent(j, carry):
        for od in range(1, D):
            for c in range(2):
                across(img_ref, od, j, c).wait_send()
        for b in range(D):
            for c in range(2):
                keep_copy(img_ref, b, j, c).wait()
        for o in range(1, S):
            scatter(j, o).wait_send()
        return carry

    lax.fori_loop(0, O, sent, 0)
    for od, os in peers:
        spread(od, os).wait_send()
    each_give(lambda c: c.wait_send())
    for o in range(1, O):
        column(o).wait_send()


def product(prob_ref, home_ref, keep_ref, out_ref, logn_ref, images, total, in_sem, out_sem):
    halves, width, wide = 2, images.shape[2], 512

    def fetch(c, n):
        cols = pl.ds(n * wide, wide)
        return pltpu.make_async_copy(
            keep_ref.at[c, :, cols], images.at[c, :, cols], in_sem.at[c, n])

    def put(c, n):
        cols = pl.ds(n * wide, wide)
        return pltpu.make_async_copy(
            total.at[c, :, cols], out_ref.at[:, c, cols], out_sem.at[c, n])

    for c in range(halves):
        for n in range(width // wide):
            fetch(c, n).start()
    logn_ref[...] = home_ref[...]
    for c in range(halves):
        for n in range(width // wide):
            fetch(c, n).wait()
            cols = slice(n * wide, (n + 1) * wide)
            total[c, :, cols] = jnp.dot(
                prob_ref[...], images[c, :, cols], preferred_element_type=jnp.float32)
            put(c, n).start()
    for c in range(halves):
        for n in range(width // wide):
            put(c, n).wait()


def shards(references, images, noise_var, shell_of, kept_blocks):
    O, D, S = (lax.axis_size(a) for a in ("orient", "dom", "shell"))
    rows = references.shape[0]
    img_rows = images.shape[0]
    local = references.shape[2]
    flat = 2 * local
    lanes = rows // S
    own = rows // D
    columns = O * img_rows
    vmem = pl.BlockSpec(memory_space=pltpu.VMEM)
    smem = pl.BlockSpec(memory_space=pltpu.SMEM)
    sem = pltpu.SemaphoreType.DMA
    f32, bf16 = jnp.float32, jnp.bfloat16
    probs, home, kept_images = pl.pallas_call(
        functools.partial(kernel, (O, D, S)),
        name="expectation",
        out_shape=(
            jax.ShapeDtypeStruct((own, D * columns), bf16),
            jax.ShapeDtypeStruct((1, img_rows), f32),
            jax.ShapeDtypeStruct((2, D, O, img_rows, local), bf16),
        ),
        in_specs=[smem, smem, vmem, pl.BlockSpec(memory_space=pl.ANY), pl.BlockSpec(memory_space=pl.ANY)],
        out_specs=(vmem, vmem, pl.BlockSpec(memory_space=pl.ANY)),
        scratch_shapes=[
            pltpu.VMEM((D, O, 2, img_rows, local), bf16),
            pltpu.VMEM((O, S, img_rows, lanes), f32),
            pltpu.VMEM((2, img_rows, rows), f32),
            pltpu.VMEM((D, columns), f32),
            pltpu.VMEM((rows, flat), bf16),
            pltpu.VMEM((D, S // D, lanes, columns), f32),
            pltpu.VMEM((rows, 2, local), bf16),
            pltpu.VMEM((img_rows, 2, local), bf16),
            pltpu.VMEM((img_rows, flat), bf16),
            pltpu.VMEM((O, S, img_rows, lanes), f32),
            pltpu.VMEM((columns, lanes), bf16),
            pltpu.VMEM((columns, lanes), f32),
            pltpu.VMEM((D, S // D, columns, lanes), bf16),
            pltpu.VMEM((D, S, 2, columns), f32),
            pltpu.VMEM((O, D, 2, columns), f32),
            pltpu.VMEM((1, local), f32),
            pltpu.VMEM((S, 1, lanes), f32),
            sem((O, 2)), sem((O, 2)), sem((O, 2)),
            sem((D, O, 2)), sem((D, O, 2)),
            sem((O, S)), sem((O, S)),
            sem((D, S)), sem((D, S)),
            sem((S,)), sem((D, S // D)),
            sem((O,)), sem((O,)), sem((D, O, 2)), sem, sem,
        ],
        compiler_params=pltpu.CompilerParams(collective_id=0, has_side_effects=True),
    )(
        kept_blocks.reshape(-1),
        noise_var,
        shell_of.reshape(1, -1),
        references,
        images,
    )
    depth = D * columns
    weighted, log_norm = pl.pallas_call(
        product,
        name="product",
        out_shape=(
            jax.ShapeDtypeStruct((own, 2, local), f32),
            jax.ShapeDtypeStruct((1, img_rows), f32),
        ),
        in_specs=[vmem, vmem, pl.BlockSpec(memory_space=pl.ANY)],
        out_specs=(pl.BlockSpec(memory_space=pl.ANY), vmem),
        scratch_shapes=[
            pltpu.VMEM((2, depth, local), bf16),
            pltpu.VMEM((2, own, local), f32),
            sem((2, local // 512)),
            sem((2, local // 512)),
        ],
    )(probs, home, kept_images.reshape(2, depth, local))
    return weighted, log_norm.reshape(img_rows)


def solution(mesh):
    placed = (
        P("orient", None, "shell"),
        P(("orient", "dom"), None, "shell"),
        P(),
        P("shell"),
        P("orient", "dom", None),
    )
    return jax.shard_map(
        shards,
        mesh=mesh,
        in_specs=placed,
        out_specs=(P(("orient", "dom"), None, "shell"), P(("orient", "dom"))),
        check_vma=False,
    )
```

```python
import functools

import jax
import jax.numpy as jnp
from jax import lax
from jax.experimental import pallas as pl
from jax.experimental.pallas import tpu as pltpu
from jax.sharding import PartitionSpec as P

floor_value = -1e30
MESH = pl.DeviceIdType.MESH


def kernel(
    sizes, kept_ref, noise_ref, shell_ref, raw_ref, whole_ref, prob_ref, home_ref, keep_ref,
    images, part, accum, logn_ref, refs_ref, turned, stage, img_stage, flat_ref, recvp, ebuf, abuf, erecv, lstat, zstat, w_s, rn_s,
    up_sem, dn_sem, img_sem, dom_send, dom_recv, rs_send, rs_recv,
    st_send, st_recv, e_send, e_recv, z_send, z_recv, out_sem, raw_sem, own_sem,
):
    O, D, S = sizes
    z, d, s = lax.axis_index("orient"), lax.axis_index("dom"), lax.axis_index("shell")
    rows, _, half = raw_ref.shape
    img_rows = whole_ref.shape[0]
    lanes = rows // S
    per = S // D
    most = kept_ref.shape[0]
    owner = s // per
    slot = s % per

    def dev(a, b, c):
        return {"orient": a, "dom": b, "shell": c}

    own = pltpu.make_async_copy(whole_ref, img_stage, own_sem)
    own.start()
    fetch = pltpu.make_async_copy(raw_ref, stage, raw_sem)
    fetch.start()
    barrier = pltpu.get_barrier_semaphore()
    for ok, to in ((z < O - 1, z + 1), (z > 0, z + O - 1)):
        @pl.when(ok)
        def _():
            pl.semaphore_signal(
                barrier, inc=1, device_id=dev(lax.rem(to, O), d, s), device_id_type=MESH)

    for od in range(D):
        for os in range(S):
            if od or os:
                pl.semaphore_signal(
                    barrier, inc=1,
                    device_id=dev(z, lax.rem(d + od, D), lax.rem(s + os, S)),
                    device_id_type=MESH,
                )
    own.wait()
    x = img_stage[...]
    for c in range(2):
        flat_ref[:, c * half:(c + 1) * half] = x[:, c, :]

    def img_ref(c):
        return flat_ref.at[:, c * half:(c + 1) * half]

    near = jnp.where(z < O - 1, 1, 0) + jnp.where(z > 0, 1, 0)
    pl.semaphore_wait(barrier, near + D * S - 1)

    def halves(b, j):
        return lambda c: images.at[b, j, c]

    def up(src, j, c):
        return pltpu.make_async_remote_copy(
            src_ref=src(c), dst_ref=images.at[d, j, c], send_sem=up_sem.at[j, c],
            recv_sem=img_sem.at[j, c],
            device_id=dev(lax.rem(z + 1, O), d, s), device_id_type=MESH)

    def down(src, j, c):
        return pltpu.make_async_remote_copy(
            src_ref=src(c), dst_ref=images.at[d, j, c], send_sem=dn_sem.at[j, c],
            recv_sem=img_sem.at[j, c],
            device_id=dev(lax.rem(z + O - 1, O), d, s), device_id_type=MESH)

    def across(src, od, j, c):
        return pltpu.make_async_remote_copy(
            src_ref=src(c), dst_ref=images.at[d, j, c], send_sem=dom_send.at[od, j, c],
            recv_sem=dom_recv.at[od, j, c],
            device_id=dev(z, lax.rem(d + od, D), s), device_id_type=MESH)

    def scatter(j, o):
        to = lax.rem(s + o, S)
        return pltpu.make_async_remote_copy(
            src_ref=part.at[j, to], dst_ref=recvp.at[j, o], send_sem=rs_send.at[j, o],
            recv_sem=rs_recv.at[j, o], device_id=dev(z, d, to), device_id_type=MESH)

    @pl.when(z < O - 1)
    def _():
        for c in range(2):
            up(img_ref, z, c).start()

    @pl.when(z > 0)
    def _():
        for c in range(2):
            down(img_ref, z, c).start()

    for od in range(1, D):
        for c in range(2):
            across(img_ref, od, z, c).start()

    def keep_copy(src, b, j, c):
        return pltpu.make_async_copy(src(c), keep_ref.at[c, b, j], out_sem.at[b, j, c])

    for c in range(2):
        keep_copy(img_ref, d, z, c).start()

    shell = shell_ref[...]
    noise = jnp.ones(shell.shape, jnp.float32)
    for i in range(noise_ref.shape[0]):
        noise = jnp.where(shell == i, noise_ref[i], noise)
    w = 1.0 / noise
    w_s[...] = w

    def norm_rows(c, carry):
        r0 = pl.multiple_of(c * lanes, lanes)
        x = stage[pl.ds(r0, lanes)]
        refs_ref[pl.ds(r0, lanes), :half] = x[:, 0, :]
        refs_ref[pl.ds(r0, lanes), half:] = x[:, 1, :]
        x0 = refs_ref[pl.ds(r0, lanes), :half].astype(jnp.float32)
        x1 = refs_ref[pl.ds(r0, lanes), half:].astype(jnp.float32)
        y = (x0 * x0 + x1 * x1) * w_s[...]
        acc = y[:, :128]
        for k in range(1, y.shape[1] // 128):
            acc = acc + y[:, k * 128:(k + 1) * 128]
        rn_s[c] = 0.5 * jnp.sum(acc.T, axis=0, keepdims=True)
        return carry

    fetch.wait()
    lax.fori_loop(0, S, norm_rows, 0)

    def cross(src, c):
        scaled = (src(c)[...].astype(jnp.float32) * w_s[...]).astype(jnp.bfloat16)
        return lax.dot_general(
            scaled, refs_ref[:, c * half:(c + 1) * half], (((1,), (1,)), ((), ())),
            preferred_element_type=jnp.float32)

    def finish(full, j):
        for k in range(S):
            part[j, k] = full[:, k * lanes:(k + 1) * lanes] - rn_s[k]
        for o in range(1, S):
            scatter(j, o).start()

    def own_block():
        finish(cross(img_ref, 0) + cross(img_ref, 1), z)

    if O == 1:
        own_block()

    def arrive(block, j, c, hop, onward):
        hop(block, j, c).wait_recv()

        @pl.when(onward)
        def _():
            hop(block, j, c).start()

        for od in range(1, D):
            across(block, od, j, c).start()
        keep_copy(block, d, j, c).start()

    lane = lax.broadcasted_iota(jnp.int32, (img_rows, lanes), 1)

    def reduce_block(j):
        v = part[j, s]
        for o in range(1, S):
            scatter(j, o).wait_recv()
            v = v + recvp[j, o]
        want = jnp.full((img_rows, lanes), j, jnp.int32)
        keep = want == kept_ref[0]
        for k in range(1, most):
            keep = keep | (want == kept_ref[k])
        v = jnp.where(keep, v, floor_value)
        m = jnp.max(v, axis=1, keepdims=True)
        e = jnp.where(keep, jnp.exp(v - m), 0.0)
        total = jnp.sum(e, axis=1, keepdims=True)
        at = pl.ds(pl.multiple_of(j * img_rows, img_rows), img_rows)
        ebuf[at, :] = e.astype(jnp.bfloat16)
        abuf[at, :] = jnp.where(lane == 0, m, total)

    def step(t, carry):
        lo = z - t
        hi = z + t
        for c in range(2):
            @pl.when(lo >= 0)
            def _():
                arrive(halves(d, lo), lo, c, up, z < O - 1)

            @pl.when(hi < O)
            def _():
                arrive(halves(d, hi), hi, c, down, z > 0)

            if c == 0:
                pl.when(t == 1)(own_block)

            for side, j, ok in ((0, lo, lo >= 0), (1, hi, hi < O)):
                @pl.when(ok)
                def _():
                    full = cross(halves(d, j), c)
                    if c == 0:
                        accum[side] = full
                    else:
                        finish(accum[side] + full, j)

            if c == 1:
                @pl.when(lo + 1 >= 0)
                def _():
                    reduce_block(lo + 1)

                @pl.when((hi - 1 < O) & (t > 1))
                def _():
                    reduce_block(hi - 1)

        return carry

    lax.fori_loop(1, O, step, 0)

    @pl.when(z == O - 1)
    def _():
        reduce_block(0)

    @pl.when(z == 0)
    def _():
        reduce_block(O - 1)


    lstat[d, s] = abuf[...].T[:2, :]

    def spread(od, os):
        return pltpu.make_async_remote_copy(
            src_ref=lstat.at[d, s], dst_ref=lstat.at[d, s], send_sem=st_send.at[od, os],
            recv_sem=st_recv.at[od, os],
            device_id=dev(z, lax.rem(d + od, D), lax.rem(s + os, S)), device_id_type=MESH)

    peers = [(od, os) for od in range(D) for os in range(S) if od or os]
    for od, os in peers:
        spread(od, os).start()

    def give(to):
        return pltpu.make_async_remote_copy(
            src_ref=ebuf, dst_ref=erecv.at[d, slot], send_sem=e_send.at[to],
            recv_sem=e_recv.at[d, slot], device_id=dev(z, owner, to), device_id_type=MESH)

    def each_give(act):
        for to in range(S):
            @pl.when((owner != d) | (s != to))
            def _():
                act(give(to))

    each_give(lambda c: c.start())

    @pl.when(owner == d)
    def _():
        erecv[d, slot] = ebuf[...]

    for od, os in peers:
        spread(od, os).wait_recv()
    for b in range(D):
        m = lstat[b, 0, 0:1, :]
        for k in range(1, S):
            m = jnp.maximum(m, lstat[b, k, 0:1, :])
        total = jnp.zeros_like(m)
        for k in range(S):
            total = total + lstat[b, k, 1:2, :] * jnp.exp(lstat[b, k, 0:1, :] - m)
        zstat[z, b, 0:1, :] = m
        zstat[z, b, 1:2, :] = total

    def column(o):
        return pltpu.make_async_remote_copy(
            src_ref=zstat.at[z], dst_ref=zstat.at[z], send_sem=z_send.at[o], recv_sem=z_recv.at[o],
            device_id=dev(lax.rem(z + o, O), d, s), device_id_type=MESH)

    for o in range(1, O):
        column(o).start()
    def dom_wait(j, carry):
        for od in range(1, D):
            b = lax.rem(d + D - od, D)
            for c in range(2):
                across(halves(d, j), od, j, c).wait_recv()
                keep_copy(halves(b, j), b, j, c).start()
        return carry

    lax.fori_loop(0, O, dom_wait, 0)

    for q in range(per):
        for b in range(D):
            @pl.when((d * per + q != s) | (d != b))
            def _():
                pltpu.make_async_remote_copy(
                    src_ref=ebuf, dst_ref=erecv.at[b, q], send_sem=e_send.at[0],
                    recv_sem=e_recv.at[b, q], device_id=dev(z, lax.rem(d + 1, D), s),
                    device_id_type=MESH).wait_recv()
    for q in range(per):
        for b in range(D):
            turned[b, q] = erecv[b, q].astype(jnp.float32).T

    for o in range(1, O):
        column(o).wait_recv()
    for b in range(D):
        m = zstat[0, b, 0:1, :]
        for k in range(1, O):
            m = jnp.maximum(m, zstat[k, b, 0:1, :])
        total = jnp.zeros_like(m)
        for k in range(O):
            total = total + zstat[k, b, 1:2, :] * jnp.exp(zstat[k, b, 0:1, :] - m)
        logn_ref[b:b + 1, :] = m + jnp.log(total)

    home = logn_ref[pl.ds(d, 1), :]
    pick = home[:, :img_rows]
    for j in range(1, O):
        pick = jnp.where(z == j, home[:, j * img_rows:(j + 1) * img_rows], pick)
    home_ref[...] = pick


    depth = O * img_rows
    for q in range(per):
        for b in range(D):
            scale = jnp.exp(lstat[b, d * per + q, 0:1, :] - logn_ref[b:b + 1, :])
            p = (turned[b, q] * scale).astype(jnp.bfloat16)
            prob_ref[q * lanes:(q + 1) * lanes, b * depth:(b + 1) * depth] = p

    @pl.when(z < O - 1)
    def _():
        def done(j, carry):
            @pl.when(j <= z)
            def _():
                for c in range(2):
                    up(img_ref, j, c).wait_send()
            return carry
        lax.fori_loop(0, O, done, 0)

    @pl.when(z > 0)
    def _():
        def done(j, carry):
            @pl.when(j >= z)
            def _():
                for c in range(2):
                    down(img_ref, j, c).wait_send()
            return carry
        lax.fori_loop(0, O, done, 0)

    def sent(j, carry):
        for od in range(1, D):
            for c in range(2):
                across(img_ref, od, j, c).wait_send()
        for b in range(D):
            for c in range(2):
                keep_copy(img_ref, b, j, c).wait()
        for o in range(1, S):
            scatter(j, o).wait_send()
        return carry

    lax.fori_loop(0, O, sent, 0)
    for od, os in peers:
        spread(od, os).wait_send()
    each_give(lambda c: c.wait_send())
    for o in range(1, O):
        column(o).wait_send()


def product(prob_ref, home_ref, keep_ref, out_ref, logn_ref, images, total, in_sem, out_sem):
    halves, width, wide = 2, images.shape[2], 512

    def fetch(c, n):
        cols = pl.ds(n * wide, wide)
        return pltpu.make_async_copy(
            keep_ref.at[c, :, cols], images.at[c, :, cols], in_sem.at[c, n])

    def put(c, n):
        cols = pl.ds(n * wide, wide)
        return pltpu.make_async_copy(
            total.at[c, :, cols], out_ref.at[:, c, cols], out_sem.at[c, n])

    for c in range(halves):
        for n in range(width // wide):
            fetch(c, n).start()
    logn_ref[...] = home_ref[...]
    for c in range(halves):
        for n in range(width // wide):
            fetch(c, n).wait()
            cols = slice(n * wide, (n + 1) * wide)
            total[c, :, cols] = jnp.dot(
                prob_ref[...], images[c, :, cols], preferred_element_type=jnp.float32)
            put(c, n).start()
    for c in range(halves):
        for n in range(width // wide):
            put(c, n).wait()


def shards(references, images, noise_var, shell_of, kept_blocks):
    O, D, S = (lax.axis_size(a) for a in ("orient", "dom", "shell"))
    rows = references.shape[0]
    img_rows = images.shape[0]
    local = references.shape[2]
    flat = 2 * local
    lanes = rows // S
    own = rows // D
    columns = O * img_rows
    vmem = pl.BlockSpec(memory_space=pltpu.VMEM)
    smem = pl.BlockSpec(memory_space=pltpu.SMEM)
    sem = pltpu.SemaphoreType.DMA
    f32, bf16 = jnp.float32, jnp.bfloat16
    probs, home, kept_images = pl.pallas_call(
        functools.partial(kernel, (O, D, S)),
        name="expectation",
        out_shape=(
            jax.ShapeDtypeStruct((own, D * columns), bf16),
            jax.ShapeDtypeStruct((1, img_rows), f32),
            jax.ShapeDtypeStruct((2, D, O, img_rows, local), bf16),
        ),
        in_specs=[smem, smem, vmem, pl.BlockSpec(memory_space=pl.ANY), pl.BlockSpec(memory_space=pl.ANY)],
        out_specs=(vmem, vmem, pl.BlockSpec(memory_space=pl.ANY)),
        scratch_shapes=[
            pltpu.VMEM((D, O, 2, img_rows, local), bf16),
            pltpu.VMEM((O, S, img_rows, lanes), f32),
            pltpu.VMEM((2, img_rows, rows), f32),
            pltpu.VMEM((D, columns), f32),
            pltpu.VMEM((rows, flat), bf16),
            pltpu.VMEM((D, S // D, lanes, columns), f32),
            pltpu.VMEM((rows, 2, local), bf16),
            pltpu.VMEM((img_rows, 2, local), bf16),
            pltpu.VMEM((img_rows, flat), bf16),
            pltpu.VMEM((O, S, img_rows, lanes), f32),
            pltpu.VMEM((columns, lanes), bf16),
            pltpu.VMEM((columns, lanes), f32),
            pltpu.VMEM((D, S // D, columns, lanes), bf16),
            pltpu.VMEM((D, S, 2, columns), f32),
            pltpu.VMEM((O, D, 2, columns), f32),
            pltpu.VMEM((1, local), f32),
            pltpu.VMEM((S, 1, lanes), f32),
            sem((O, 2)), sem((O, 2)), sem((O, 2)),
            sem((D, O, 2)), sem((D, O, 2)),
            sem((O, S)), sem((O, S)),
            sem((D, S)), sem((D, S)),
            sem((S,)), sem((D, S // D)),
            sem((O,)), sem((O,)), sem((D, O, 2)), sem, sem,
        ],
        compiler_params=pltpu.CompilerParams(collective_id=0, has_side_effects=True),
    )(
        kept_blocks.reshape(-1),
        noise_var,
        shell_of.reshape(1, -1),
        references,
        images,
    )
    depth = D * columns
    weighted, log_norm = pl.pallas_call(
        product,
        name="product",
        out_shape=(
            jax.ShapeDtypeStruct((own, 2, local), f32),
            jax.ShapeDtypeStruct((1, img_rows), f32),
        ),
        in_specs=[vmem, vmem, pl.BlockSpec(memory_space=pl.ANY)],
        out_specs=(pl.BlockSpec(memory_space=pl.ANY), vmem),
        scratch_shapes=[
            pltpu.VMEM((2, depth, local), bf16),
            pltpu.VMEM((2, own, local), f32),
            sem((2, local // 512)),
            sem((2, local // 512)),
        ],
    )(probs, home, kept_images.reshape(2, depth, local))
    return weighted, log_norm.reshape(img_rows)


def solution(mesh):
    placed = (
        P("orient", None, "shell"),
        P(("orient", "dom"), None, "shell"),
        P(),
        P("shell"),
        P("orient", "dom", None),
    )
    return jax.shard_map(
        shards,
        mesh=mesh,
        in_specs=placed,
        out_specs=(P(("orient", "dom"), None, "shell"), P(("orient", "dom"))),
        check_vma=False,
    )
```
